512 devices in a mesh: dp: 128 (over z, y, core), head: 4 (over x).
Axes of the slice: x: 4, y: 8, z: 8, core: 2. Of those that a mesh axis runs over, the one named last changes fastest.
Arguments:
- queries: bfloat16 [32768, 1536], P(('dp', 'head')), may hold values from -100 to 100
- fresh_keyvals: bfloat16 [32768, 512], P(('dp', 'head')), may hold values from -4.1 to 4.1
- ssm_input: bfloat16 [32768, 3072], P(('dp', 'head')), may hold values from -4 to 4
- gate_input: bfloat16 [32768, 3072], P(('dp', 'head')), may hold values from -40 to 40
- state_maps: bfloat16 [32768, 512], P(('dp', 'head')), may hold values from -4 to 4
- step_logit: bfloat16 [32768, 24], P(('dp', 'head')), may hold values from -6 to 8
- slot_mask: int32 [32768], P(('dp', 'head')), may hold values 0 or 1
- cache_pool: bfloat16 [16384, 32, 256], P('dp', 'head'), may hold values from -4 to 4
- page_map: int32 [128, 128], P('dp'), may hold values from 0 to 127, each once within a row
- cached_lengths: int32 [128], P('dp'), may hold values from 1 to 2048, 131072 in all
- prior_state: bfloat16 [128, 24, 128, 256], P('dp', 'head'), may hold values from -0.8984375 to 0.8984375
- decay_log: float32 [24], P('head'), may hold values from -4.61 to 0.7
- step_bias: float32 [24], P('head'), may hold values from -1 to 1
- skip_gain: float32 [24], P('head'), may hold values from 0.5 to 1.5
- norm_gain: float32 [3072], replicated, may hold values from 0.1 to 1.9
Outputs:
- mixed: bfloat16 [32768, 4608], P(('dp', 'head'))
The draws below stay inside these ranges and needn't reach their ends.
Inputs may be any that keep to these rules, and one draw needn't show every extreme that they name: `page_map`: each row is a permutation of 0 to 127. `cached_lengths`: the lengths sum to 131072; the largest is exactly 2048.
All inputs are finite; a program needn't handle non-finite values. No bound on the sum of `slot_mask` or of `cached_lengths` on one device may be relied on, other than what follows from the above.
Results may differ from the reference program's by a relative error of at most 0.012.
Values may be sent and summed in bfloat16 or wider, within the bound.
A program may use at most 64 MiB of HBM per device.

```python
import math
import jax
import jax.numpy as jnp
import numpy as np
from jax import lax

HD = 128
QH = 12
KVH = 2
MAMBA_HEADS = 24
MD = 128
STATE = 256
SPAN = 256
MI = 3072
REQUESTS = 128
TOKEN_SLOTS = 32768
MAXLEN = 2048
HALF = 8
N_DP = 128


def attention_streams(key):
    base_keys = jnp.clip(jax.random.normal(jax.random.fold_in(key, 11), (TOKEN_SLOTS, KVH, HD), jnp.float32), -4.0, 4.0)
    base_values = jnp.clip(jax.random.normal(jax.random.fold_in(key, 12), (TOKEN_SLOTS, KVH, HD), jnp.float32), -4.0, 4.0)
    base_queries = 2.5 * jnp.clip(jax.random.normal(jax.random.fold_in(key, 13), (TOKEN_SLOTS, QH, HD), jnp.float32), -4.0, 4.0)
    return (base_queries, base_keys, base_values)


def draw_queries(key, part):
    base_queries, base_keys, base_values = attention_streams(key)
    return base_queries.reshape(TOKEN_SLOTS, QH * HD).astype(jnp.bfloat16)


def draw_fresh_keyvals(key, part):
    base_queries, base_keys, base_values = attention_streams(key)
    stacked = jnp.stack([base_keys, base_values], axis=2)
    return stacked.reshape(TOKEN_SLOTS, 2 * KVH * HD).astype(jnp.bfloat16)


def draw_gate_input(key, part):
    noise = jnp.clip(jax.random.normal(jax.random.fold_in(key, 21), (TOKEN_SLOTS, MI), jnp.float32), -4.0, 4.0)
    row_scale = jnp.exp(jax.random.uniform(jax.random.fold_in(key, 22), (TOKEN_SLOTS, 1), jnp.float32, 0.0, 1.15))
    column_scale = jnp.exp(jax.random.uniform(jax.random.fold_in(key, 23), (1, MI), jnp.float32, 0.0, 1.15))
    return (noise * row_scale * column_scale).astype(jnp.bfloat16)


def draw_step_logit(key, part):
    start_offset = jnp.clip(jax.random.normal(jax.random.fold_in(key, 31), (TOKEN_SLOTS, MAMBA_HEADS), jnp.float32), -4.0, 4.0) * 0.5 - 4.0
    request_spans = jax.random.randint(jax.random.fold_in(key, 32), (TOKEN_SLOTS, MAMBA_HEADS), 0, 200) == 0
    return jnp.where(request_spans, start_offset + 10.0, start_offset).astype(jnp.bfloat16)


def draw_decay_log(key, part):
    values = jax.random.uniform(jax.random.fold_in(key, 41), (MAMBA_HEADS,), jnp.float32, -3.5, 0.69)
    return values


def with_ends(array, key, least, top_value):
    index_at = [jax.random.randint(jax.random.fold_in(key, axis), (), 0, length) for axis, length in enumerate(array.shape)]
    main_axis = array.shape.index(max(array.shape))
    beside = index_at[:main_axis] + [(index_at[main_axis] + 1) % array.shape[main_axis]] + index_at[main_axis + 1:]
    return array.at[tuple(index_at)].set(least).at[tuple(beside)].set(top_value)


def levels(rng, dims, cuts, low, high):
    loudness, own = 1.0, jax.random.fold_in(rng, 6)
    for axis_at, shards_of in cuts:
        steps = jnp.exp(jax.random.uniform(jax.random.fold_in(own, axis_at), (shards_of,), jnp.float32, low / len(cuts), high / len(cuts)))
        loudness = loudness * jnp.repeat(steps, dims[axis_at] // shards_of).reshape([-1 if axis == axis_at else 1 for axis in range(len(dims))])
    return loudness


def length_profile(number_of, total, limit, lean):
    portions = [(1 << 20) // math.isqrt(rank ** lean) + 1 for rank in range(2, number_of + 1)]
    spare, holding = total - limit - (number_of - 1), [1] * (number_of - 1)
    while spare > 0:
        candidates = [i for i in range(number_of - 1) if holding[i] < limit]
        mass, budget = sum([portions[i] for i in candidates]), spare
        for i in candidates:
            extra = min(limit - holding[i], max(1, budget * portions[i] // mass), spare)
            holding[i] = holding[i] + extra
            spare = spare - extra
    return np.array([limit] + holding)


def ragged_sizes(rng, count, total, limit, lean):
    if count == 2:
        one = jax.random.randint(rng, (), max(1, total - limit), min(limit, total - 1) + 1)
        return jnp.stack([one, total - one])
    tallies = jnp.asarray(length_profile(count, total, limit, lean), jnp.int32)
    couples = (count - 1) // 2
    source_of, sink = tallies[1:1 + 2 * couples:2], tallies[2:2 + 2 * couples:2]
    margin = jnp.minimum(source_of - 1, limit - sink)
    shifted = jax.random.randint(jax.random.fold_in(rng, 1), (couples,), 0, 1 << 20) % (margin + 1)
    tallies = tallies.at[1:1 + 2 * couples:2].set(source_of - shifted).at[2:2 + 2 * couples:2].set(sink + shifted)
    return tallies[jax.random.permutation(jax.random.fold_in(rng, 2), count)]


def centred(rng, extent, deviation, bound, shards=(), kind=jnp.bfloat16):
    array = deviation * jax.random.normal(rng, extent, jnp.float32)
    if shards:
        array = array * levels(rng, extent, shards, -0.22, 0.18)
    return jnp.clip(array, -bound, bound).astype(kind)


def setup_inputs(seed: int = 0) -> dict:
    key_of = jax.random.split(jax.random.key(seed), 16)
    queries = draw_queries(jax.random.fold_in(key_of[15], 71), 0)
    fresh_keyvals = draw_fresh_keyvals(jax.random.fold_in(key_of[15], 71), 0)
    ssm_input = centred(key_of[2], (TOKEN_SLOTS, MI), 1.0, 4.0, ((0, 512),))
    gate_input = draw_gate_input(jax.random.fold_in(key_of[15], 71), 0)
    state_maps = centred(key_of[4], (TOKEN_SLOTS, 2 * STATE), 1.0, 4.0, ((0, 512),))
    step_logit = draw_step_logit(jax.random.fold_in(key_of[15], 71), 0)
    slot_mask = with_ends((jax.random.randint(key_of[6], (TOKEN_SLOTS,), 0, 8) < 7).astype(jnp.int32), jax.random.fold_in(key_of[6], 1), 0, 1)
    cache_pool = centred(key_of[7], (N_DP * REQUESTS, 2 * KVH * HALF, 2 * HD), 1.0, 4.0, ((0, 128), (1, 4)))
    page_map = jax.vmap(lambda own: jax.random.permutation(own, N_DP))(jax.random.split(key_of[8], REQUESTS)).reshape((REQUESTS, N_DP)).astype(jnp.int32)
    cached_lengths = ragged_sizes(key_of[9], REQUESTS, REQUESTS * MAXLEN // 2, MAXLEN, 1).astype(jnp.int32)
    prior_state = centred(key_of[10], (REQUESTS, MAMBA_HEADS, MD, STATE), 0.15, 0.8984375, ((0, 128), (1, 4)))
    decay_log = draw_decay_log(jax.random.fold_in(key_of[15], 71), 0)
    step_bias = jnp.clip(jax.random.uniform(key_of[12], (MAMBA_HEADS,), jnp.float32, -1.0, 1.0) * levels(key_of[12], (MAMBA_HEADS,), ((0, 4),), -0.4, 0.0), -1.0, 1.0)
    skip_gain = jnp.clip(0.5 + 1.0 * jax.random.uniform(key_of[13], (MAMBA_HEADS,), jnp.float32) ** levels(key_of[13], (MAMBA_HEADS,), ((0, 4),), -0.2, 0.2), 0.5, 1.5)
    norm_gain = jnp.clip(1.0 + 0.18 * jax.random.normal(key_of[14], (MI,), jnp.float32), 0.1, 1.9)
    return dict(queries=queries, fresh_keyvals=fresh_keyvals, ssm_input=ssm_input, gate_input=gate_input, state_maps=state_maps, step_logit=step_logit, slot_mask=slot_mask, cache_pool=cache_pool, page_map=page_map, cached_lengths=cached_lengths, prior_state=prior_state, decay_log=decay_log, step_bias=step_bias, skip_gain=skip_gain, norm_gain=norm_gain)


HIGHEST = lax.Precision.HIGHEST
EPSILON = 1e-05

def attention(query_rows, all_keys, all_values, cached_count, valid_rows):
    length = query_rows.shape[0]
    key_count = all_keys.shape[0]
    cached_positions = key_count - length
    row_block = min(512, length)
    inv_scale = 1.0 / math.sqrt(HD)
    key_slots = jnp.arange(key_count, dtype=jnp.int32)
    new_index = key_slots - cached_positions
    live_new = jnp.concatenate([jnp.zeros((cached_positions,), dtype=bool), valid_rows])
    key_live = jnp.where(key_slots < cached_positions, key_slots < cached_count, live_new)
    results = []
    for head_num in range(query_rows.shape[1] // HD):
        pieces = []
        for offset in range(0, length, row_block):
            block_query = query_rows[offset:offset + row_block, head_num * HD:(head_num + 1) * HD]
            row_ids = offset + jnp.arange(row_block, dtype=jnp.int32)
            allowed = key_live[None, :] & ((key_slots[None, :] < cached_positions) | (new_index[None, :] <= row_ids[:, None]))
            scores = jnp.dot(block_query, all_keys.T, preferred_element_type=jnp.float32) * inv_scale
            scores = jnp.where(allowed, scores, -jnp.inf)
            row_max = lax.optimization_barrier(jnp.max(scores, axis=1, keepdims=True))
            exp_terms = jnp.exp(scores - row_max)
            row_total = lax.optimization_barrier(jnp.sum(exp_terms, axis=1, keepdims=True))
            weighted_values = jnp.dot(exp_terms.astype(jnp.bfloat16), all_values, preferred_element_type=jnp.float32)
            pieces.append(weighted_values / row_total)
        results.append(jnp.concatenate(pieces, axis=0))
    joined = jnp.concatenate(results, axis=1) * valid_rows[:, None].astype(jnp.float32)
    return joined.astype(jnp.bfloat16)

def block_scan(inputs, in_raw, out_raw, steps, log_decay, carried):
    length = inputs.shape[0]
    block_len = min(128, length)
    causal = jnp.arange(block_len)[:, None] >= jnp.arange(block_len)[None, :]
    outputs = []
    for offset in range(0, length, block_len):
        block_input = inputs[offset:offset + block_len]
        block_in_raw = in_raw[offset:offset + block_len]
        block_out_raw = out_raw[offset:offset + block_len]
        block_in_map = block_in_raw.astype(jnp.float32)
        block_out_map = block_out_raw.astype(jnp.float32)
        block_steps = steps[offset:offset + block_len]
        cumulative = jnp.cumsum(log_decay[offset:offset + block_len], axis=0)
        log_gaps = cumulative[:, None, :] - cumulative[None, :, :]
        decays = jnp.exp(jnp.where(causal[:, :, None], log_gaps, -jnp.inf))
        intersections = jnp.dot(block_out_raw, block_in_raw.T, preferred_element_type=jnp.float32)
        weights = intersections[:, :, None] * decays * block_steps[None, :, :]
        within = jnp.einsum('tsh,shp->thp', weights, block_input, precision=HIGHEST)
        from_state = jnp.einsum('tn,hpn->thp', block_out_map, carried, precision=HIGHEST) * jnp.exp(cumulative)[:, :, None]
        outputs.append(within + from_state)
        tail_weight = jnp.exp(cumulative[-1:, :] - cumulative) * block_steps
        carried = carried * jnp.exp(cumulative[-1])[:, None, None] + jnp.einsum('shp,sn->hpn', block_input * tail_weight[:, :, None], block_in_map, precision=HIGHEST)
    return jnp.concatenate(outputs, axis=0)

def state_space(inputs, maps, step_rows, valid_rows, decay_log, step_bias, skip_gain, prior):
    length = inputs.shape[0]
    head_count = decay_log.shape[0]
    valid_float = valid_rows.astype(jnp.float32)
    steps = jax.nn.softplus(step_rows.astype(jnp.float32) + step_bias[None, :]) * valid_float[:, None]
    log_decay = -jnp.exp(decay_log)[None, :] * steps
    input_float = inputs.astype(jnp.float32).reshape(length, head_count, -1)
    in_raw = maps[:, :STATE]
    out_raw = maps[:, STATE:]
    result = block_scan(input_float, in_raw, out_raw, steps, log_decay, prior.astype(jnp.float32))
    result = (result + skip_gain[None, :, None] * input_float) * valid_float[:, None, None]
    return result.reshape(length, -1).astype(jnp.bfloat16)

def reference(queries, fresh_keyvals, ssm_input, gate_input, state_maps, step_logit, slot_mask, cache_pool, page_map, cached_lengths, prior_state, decay_log, step_bias, skip_gain, norm_gain):
    pool = cache_pool.reshape(REQUESTS, REQUESTS, KVH, 2, HALF, 2 * HD)
    group_size = QH // KVH

    def one_request(request):
        first_row = (request * SPAN).astype(jnp.int32)
        query_rows = lax.dynamic_slice_in_dim(queries, first_row, SPAN, 0)
        keyval_rows = lax.dynamic_slice_in_dim(fresh_keyvals, first_row, SPAN, 0)
        input_rows = lax.dynamic_slice_in_dim(ssm_input, first_row, SPAN, 0)
        gate_rows = lax.dynamic_slice_in_dim(gate_input, first_row, SPAN, 0)
        map_rows = lax.dynamic_slice_in_dim(state_maps, first_row, SPAN, 0)
        step_rows = lax.dynamic_slice_in_dim(step_logit, first_row, SPAN, 0)
        valid_rows = lax.dynamic_slice_in_dim(slot_mask, first_row, SPAN, 0) > 0
        holders = lax.dynamic_index_in_dim(page_map, request, 0, keepdims=False)
        pool_rows = lax.dynamic_index_in_dim(pool, request, 1, keepdims=False)
        page_rows = jnp.take(pool_rows, holders, axis=0)
        cached_count = lax.dynamic_index_in_dim(cached_lengths, request, 0, keepdims=False)
        prior = lax.dynamic_index_in_dim(prior_state, request, 0, keepdims=False)
        attended_parts = []
        for group in range(KVH):
            cache_rows = page_rows[:, group].reshape(MAXLEN, 2 * HD)
            all_keys = jnp.concatenate([cache_rows[:, :HD], keyval_rows[:, 2 * group * HD:(2 * group + 1) * HD]], axis=0)
            all_values = jnp.concatenate([cache_rows[:, HD:], keyval_rows[:, (2 * group + 1) * HD:(2 * group + 2) * HD]], axis=0)
            group_queries = query_rows[:, group * group_size * HD:(group + 1) * group_size * HD]
            attended_parts.append(attention(group_queries, all_keys, all_values, cached_count, valid_rows))
        attended = jnp.concatenate(attended_parts, axis=1)
        scanned = state_space(input_rows, map_rows, step_rows, valid_rows, decay_log, step_bias, skip_gain, prior)
        gated = scanned.astype(jnp.float32) * jax.nn.silu(gate_rows.astype(jnp.float32))
        normed = gated * lax.rsqrt(lax.optimization_barrier(jnp.mean(gated * gated, axis=1, keepdims=True)) + EPSILON) * norm_gain[None, :]
        return jnp.concatenate([attended, normed.astype(jnp.bfloat16)], axis=1)
    stacked = lax.map(one_request, jnp.arange(REQUESTS, dtype=jnp.int32))
    return stacked.reshape(TOKEN_SLOTS, QH * HD + MI)
```

```python
import math

import jax
import jax.numpy as jnp
from jax import lax
from jax.experimental import pallas as pl
from jax.experimental.pallas import tpu as pltpu
from jax.sharding import PartitionSpec as P

HD = 128
QH = 12
STATE = 256
MI = 3072
EPSILON = 1e-05
NX = 4
NDP = 128
NY = 8
NZ = 8
TOK = 64
SPAN = 256
GW = 768
CACHED = 1024
FRESH = 128
MASK_LANE = 24
NEG = -1e30
LOG2E = 1.4426950408889634
SCALE = LOG2E / math.sqrt(HD)
MESH = pl.DeviceIdType.MESH
F32 = jnp.float32
BF16 = jnp.bfloat16
AUX, MAPS, XS, KV, Q, SCAN, ATT, LSE = range(8)


def iota(shape, axis):
    return lax.broadcasted_iota(jnp.int32, shape, axis)


def dot_nt(a, b):
    return lax.dot_general(a, b, (((1,), (1,)), ((), ())), preferred_element_type=F32)


def dot_nn(a, b):
    return jnp.dot(a, b, preferred_element_type=F32)


def kernel(
    q, kv, xs, gate, maps, logit, mask, pool, page_map, length, prior, decay_log, step_bias,
    skip_gain, norm_gain, out,
    aux_own, aux_r, maps_r, xs_r, kv_r, q_r, pages, prior_v, gate_v, scan_s, scan_r, att_s, att_r,
    lse_s, lse_r, keys, values, send_sem, recv_sem, page_send, page_recv, local_sem, entry_sem,
    pair_sem,
):
    d = lax.axis_index("dp")
    h = lax.axis_index("head")
    z, y, c = d // (2 * NY), (d // 2) % NY, d % 2
    g, half = h // 2, h % 2
    barrier = pltpu.get_barrier_semaphore()

    def y_peer(k):
        return z * (2 * NY) + ((y + k) % NY) * 2 + c

    def z_peer(k):
        return ((z + k) % NZ) * (2 * NY) + y * 2 + c

    partner = d + 1 - 2 * c
    for k in range(1, NX):
        pl.semaphore_signal(barrier, 1, device_id=(d, (h + k) % NX), device_id_type=MESH)
    pl.semaphore_signal(barrier, 1, device_id=(partner, h), device_id_type=MESH)
    for k in range(1, NY):
        pl.semaphore_signal(barrier, 1, device_id=(y_peer(k), h), device_id_type=MESH)
    for k in range(1, NZ):
        pl.semaphore_signal(barrier, 1, device_id=(z_peer(k), h), device_id_type=MESH)

    def group_cols(ref, index):
        return ref.at[:, pl.ds(pl.multiple_of(index * GW, 128), GW)]

    def fresh_part(index):
        return kv.at[
            pl.ds(pl.multiple_of((index % 2) * 32, 32), 32),
            pl.ds(pl.multiple_of((index // 2) * 256, 128), 256),
        ]

    locals_ = [
        pltpu.make_async_copy(maps, maps_r.at[h], local_sem.at[0]),
        pltpu.make_async_copy(group_cols(xs, h), xs_r.at[h], local_sem.at[1]),
        pltpu.make_async_copy(fresh_part(h), kv_r.at[h], local_sem.at[2]),
        pltpu.make_async_copy(group_cols(q, g), q_r.at[h], local_sem.at[3]),
        pltpu.make_async_copy(pool.at[d], pages.at[d], local_sem.at[4]),
        pltpu.make_async_copy(prior, prior_v, local_sem.at[5]),
        pltpu.make_async_copy(gate, gate_v, local_sem.at[6]),
    ]
    for copy in locals_:
        copy.start()

    eye = iota((TOK, TOK), 0) == iota((TOK, TOK), 1)
    own_mask = jnp.where(eye, jnp.broadcast_to(mask[...].astype(F32), (TOK, TOK)), 0.0)
    own_mask = jnp.sum((own_mask > 0.5).astype(F32), axis=1, keepdims=True)
    spread = (iota((24, 128), 0) == iota((24, 128), 1)).astype(BF16)
    aux = lax.dot_general(
        logit[...], spread, (((0,), (0,)), ((), ())), preferred_element_type=F32
    )
    aux = jnp.where(iota((TOK, 128), 1) == MASK_LANE, own_mask, aux).astype(BF16)
    aux_own[...] = aux
    aux_r[h] = aux

    pl.semaphore_wait(barrier, NX - 1 + 1 + NY - 1 + NZ - 1)

    def remote(kind, k, src, dst):
        return pltpu.make_async_remote_copy(
            src_ref=src,
            dst_ref=dst,
            send_sem=send_sem.at[kind, k],
            recv_sem=recv_sem.at[kind, k],
            device_id=(d, (h + k) % NX),
            device_id_type=MESH,
        )

    order = (1, 3, 2)
    sends = {}
    for k in order:
        sends[AUX, k] = remote(AUX, k, aux_own, aux_r.at[h])
    for k in order:
        sends[MAPS, k] = remote(MAPS, k, maps, maps_r.at[h])
    for k in order:
        sends[XS, k] = remote(XS, k, group_cols(xs, (h + k) % NX), xs_r.at[h])
    for k in order:
        sends[KV, k] = remote(KV, k, fresh_part((h + k) % NX), kv_r.at[h])
    for k in order:
        sends[Q, k] = remote(Q, k, group_cols(q, ((h + k) % NX) // 2), q_r.at[h])
    for copy in sends.values():
        copy.start()

    for k in range(1, NY):
        pl.semaphore_signal(entry_sem, 1, device_id=(y_peer(k), h), device_id_type=MESH)
    pl.semaphore_wait(entry_sem, NY - 1)
    pl.semaphore_signal(pair_sem, 1, device_id=(partner, h), device_id_type=MESH)
    pl.semaphore_wait(pair_sem, 1)

    def send_page(i, carry):
        target = (d + i * 37) % NDP
        pltpu.make_async_remote_copy(
            src_ref=pool.at[target],
            dst_ref=pages.at[d],
            send_sem=page_send,
            recv_sem=page_recv,
            device_id=(target, h),
            device_id_type=MESH,
        ).start()
        return carry

    lax.fori_loop(1, NDP, send_page, 0)

    def arrive(kind):
        for k in order:
            sends[kind, k].wait_recv()

    arrive(AUX)
    aux_all = aux_r[...].reshape(SPAN, 128)
    rows, lanes = iota((128, 128), 0), iota((128, 128), 1)
    pick = ((rows == 6 * h + lanes) & (lanes < 6)).astype(BF16)
    own_logit = dot_nn(aux_all, pick)
    real = dot_nn(aux_all, (rows == MASK_LANE).astype(BF16))
    lane_row = iota((1, 128), 1)
    bias_row = jnp.zeros((1, 128), F32)
    rate_row = jnp.zeros((1, 128), F32)
    for j in range(6):
        bias_row = jnp.where(lane_row == j, step_bias[j], bias_row)
        rate_row = jnp.where(lane_row == j, decay_log[j], rate_row)
    rate_row = jnp.where(lane_row < 6, -jnp.exp(rate_row), 0.0)
    v = own_logit + bias_row
    steps = (jnp.maximum(v, 0.0) + jnp.log(1.0 + jnp.exp(-jnp.abs(v)))) * real
    log_decay = steps * rate_row
    causal = iota((SPAN, SPAN), 0) >= iota((SPAN, SPAN), 1)
    cumulative = jnp.dot(
        causal.astype(F32), log_decay, precision=lax.Precision.HIGHEST, preferred_element_type=F32
    )
    cumulative_t = cumulative.T
    steps_t = steps.T
    carry_weight = jnp.exp(cumulative)

    locals_[0].wait()
    locals_[5].wait()
    arrive(MAPS)
    in_map = maps_r[:, :, 0:STATE].reshape(SPAN, STATE)
    out_map = maps_r[:, :, STATE : 2 * STATE].reshape(SPAN, STATE)
    inter = dot_nt(out_map, in_map)
    locals_[1].wait()
    arrive(XS)
    for j in range(6):
        cols = pl.ds(j * HD, HD)
        gap = cumulative[:, j : j + 1] - cumulative_t[j : j + 1, :]
        weights = jnp.where(causal, jnp.exp(gap), 0.0) * inter * steps_t[j : j + 1, :]
        x = xs_r[:, :, cols].reshape(SPAN, HD)
        from_state = dot_nt(out_map, prior_v[pl.ds(j * HD, HD), :])
        result = dot_nn(weights.astype(BF16), x) + from_state * carry_weight[:, j : j + 1]
        result = (result + skip_gain[j] * x.astype(F32)) * real
        scan_s[:, :, cols] = result.astype(BF16).reshape(NX, TOK, HD)

    for k in order:
        sends[SCAN, k] = remote(SCAN, k, scan_s.at[(h + k) % NX], scan_r.at[h])
        sends[SCAN, k].start()

    one_hot = (page_map[...] == rows).astype(BF16)
    page_of = dot_nt(iota((8, 128), 1).astype(BF16), one_hot)
    expand = (iota((128, CACHED), 1) // 8 == iota((128, CACHED), 0)).astype(BF16)
    position = dot_nn(page_of.astype(BF16), expand)[0:1, :] * 16.0
    position = position + (half * 8 + iota((1, CACHED), 1) % 8).astype(F32)
    cache_bias = jnp.where(position < length[...].astype(F32), 0.0, NEG)
    slot_row = dot_nt((iota((8, 128), 1) == MASK_LANE).astype(BF16), aux_all)

    def slot_of(key):
        return (key // 32) * TOK + half * 32 + key % 32

    pick_slot = (iota((SPAN, FRESH), 0) == slot_of(iota((SPAN, FRESH), 1))).astype(BF16)
    real_row = dot_nn(slot_row.astype(BF16), pick_slot)[0:1, :]
    seen = (slot_of(iota((SPAN, FRESH), 1)) <= iota((SPAN, FRESH), 0)) & (real_row > 0.5)
    fresh_bias = jnp.where(seen, 0.0, NEG)

    locals_[2].wait()
    locals_[3].wait()
    arrive(KV)
    keys[pl.ds(CACHED, FRESH), :] = kv_r[:, :, 0:HD].reshape(FRESH, HD)
    values[pl.ds(CACHED, FRESH), :] = kv_r[:, :, HD : 2 * HD].reshape(FRESH, HD)
    arrive(Q)
    locals_[4].wait()
    page_wait = pltpu.make_async_remote_copy(
        src_ref=pool.at[pl.ds(0, NDP - 1)],
        dst_ref=pages.at[pl.ds(0, NDP - 1)],
        send_sem=page_send,
        recv_sem=page_recv,
        device_id=(partner, h),
        device_id_type=MESH,
    )
    page_wait.wait_recv()
    keys[pl.ds(0, CACHED), :] = pages[:, :, 0:HD].reshape(CACHED, HD)
    values[pl.ds(0, CACHED), :] = pages[:, :, HD : 2 * HD].reshape(CACHED, HD)

    lse = jnp.zeros((SPAN, 128), F32)
    for j in range(6):
        cols = pl.ds(j * HD, HD)
        query = q_r[:, :, cols].reshape(SPAN, HD)
        old = dot_nt(query, keys[pl.ds(0, CACHED), :]) + cache_bias
        new = dot_nt(query, keys[pl.ds(CACHED, FRESH), :]) + fresh_bias
        top = jnp.maximum(
            jnp.max(old, axis=1, keepdims=True), jnp.max(new, axis=1, keepdims=True)
        )
        old = jnp.exp2((old - top) * SCALE)
        new = jnp.exp2((new - top) * SCALE)
        total = jnp.sum(old, axis=1, keepdims=True) + jnp.sum(new, axis=1, keepdims=True)
        weighted = dot_nn(old.astype(BF16), values[pl.ds(0, CACHED), :])
        weighted = weighted + dot_nn(new.astype(BF16), values[pl.ds(CACHED, FRESH), :])
        att_s[:, :, cols] = (weighted / total).astype(BF16).reshape(NX, TOK, HD)
        lse = jnp.where(iota((SPAN, 128), 1) == j, top * SCALE + jnp.log2(total), lse)
    for u in range(NX):
        lse_s[u] = lse[u * TOK : (u + 1) * TOK, :].T[0:8, :]

    for k in order:
        sends[LSE, k] = remote(LSE, k, lse_s.at[(h + k) % NX], lse_r.at[h])
        sends[LSE, k].start()
        sends[ATT, k] = remote(ATT, k, att_s.at[(h + k) % NX], att_r.at[h])
        sends[ATT, k].start()

    locals_[6].wait()
    scan_r[h] = scan_s[h]
    arrive(SCAN)
    squares = jnp.zeros((TOK, 1), F32)
    for u in range(NX):
        z_in = gate_v[:, pl.ds(u * GW, GW)].astype(F32)
        gated = scan_r[u].astype(F32) * (z_in / (1.0 + jnp.exp(-z_in)))
        squares = squares + jnp.sum(gated * gated, axis=1, keepdims=True)
    inverse = lax.rsqrt(squares / MI + EPSILON)
    for u in range(NX):
        z_in = gate_v[:, pl.ds(u * GW, GW)].astype(F32)
        gated = scan_r[u].astype(F32) * (z_in / (1.0 + jnp.exp(-z_in)))
        normed = gated * inverse * norm_gain[:, pl.ds(u * GW, GW)]
        out[:, pl.ds(QH * HD + u * GW, GW)] = normed.astype(BF16)

    att_r[h] = att_s[h]
    lse_r[h] = lse_s[h]
    arrive(LSE)
    arrive(ATT)
    lse_all = lse_r[...].reshape(32, TOK).T
    for group in range(2):
        a, b = 2 * group, 2 * group + 1
        for j in range(6):
            first = lse_all[:, a * 8 + j : a * 8 + j + 1]
            second = lse_all[:, b * 8 + j : b * 8 + j + 1]
            share = own_mask / (1.0 + jnp.exp2(second - first))
            rest = own_mask / (1.0 + jnp.exp2(first - second))
            cols = pl.ds(j * HD, HD)
            joined = att_r[a, :, cols].astype(F32) * share + att_r[b, :, cols].astype(F32) * rest
            out[:, pl.ds(group * GW + j * HD, HD)] = joined.astype(BF16)

    for copy in sends.values():
        copy.wait_send()
    page_wait.wait_send()


def local(
    queries, fresh_keyvals, ssm_input, gate_input, state_maps, step_logit, slot_mask, cache_pool,
    page_map, cached_lengths, prior_state, decay_log, step_bias, skip_gain, norm_gain,
):
    hbm = pl.BlockSpec(memory_space=pl.ANY)
    vmem = pl.BlockSpec(memory_space=pltpu.VMEM)
    smem = pl.BlockSpec(memory_space=pltpu.SMEM)
    return pl.pallas_call(
        kernel,
        out_shape=jax.ShapeDtypeStruct((TOK, QH * HD + MI), BF16),
        in_specs=[
            hbm, hbm, hbm, hbm, hbm, vmem, vmem, hbm, vmem, vmem, hbm, smem, smem, smem, vmem,
        ],
        out_specs=vmem,
        scratch_shapes=[
            pltpu.VMEM((TOK, 128), BF16),
            pltpu.VMEM((NX, TOK, 128), BF16),
            pltpu.VMEM((NX, TOK, 2 * STATE), BF16),
            pltpu.VMEM((NX, TOK, GW), BF16),
            pltpu.VMEM((NX, 32, 2 * HD), BF16),
            pltpu.VMEM((NX, TOK, GW), BF16),
            pltpu.VMEM((NDP, 8, 2 * HD), BF16),
            pltpu.VMEM((GW, STATE), BF16),
            pltpu.VMEM((TOK, MI), BF16),
            pltpu.VMEM((NX, TOK, GW), BF16),
            pltpu.VMEM((NX, TOK, GW), BF16),
            pltpu.VMEM((NX, TOK, GW), BF16),
            pltpu.VMEM((NX, TOK, GW), BF16),
            pltpu.VMEM((NX, 8, TOK), F32),
            pltpu.VMEM((NX, 8, TOK), F32),
            pltpu.VMEM((CACHED + FRESH, HD), BF16),
            pltpu.VMEM((CACHED + FRESH, HD), BF16),
            pltpu.SemaphoreType.DMA((8, NX)),
            pltpu.SemaphoreType.DMA((8, NX)),
            pltpu.SemaphoreType.DMA,
            pltpu.SemaphoreType.DMA,
            pltpu.SemaphoreType.DMA((7,)),
            pltpu.SemaphoreType.REGULAR,
            pltpu.SemaphoreType.REGULAR,
        ],
        compiler_params=pltpu.CompilerParams(collective_id=0, has_side_effects=True),
        name="mixer",
    )(
        queries, fresh_keyvals, ssm_input, gate_input, state_maps, step_logit.T,
        slot_mask.reshape(1, TOK), cache_pool, page_map, cached_lengths.reshape(1, 1),
        prior_state.reshape(GW, STATE), decay_log, step_bias, skip_gain, norm_gain.reshape(1, MI),
    )


def solution(mesh):
    tokens = P(("dp", "head"), None)
    in_specs = (
        tokens, tokens, tokens, tokens, tokens, tokens,
        P(("dp", "head")),
        P("dp", "head", None),
        P("dp", None),
        P("dp"),
        P("dp", "head", None, None),
        P("head"), P("head"), P("head"),
        P(),
    )
    return jax.shard_map(
        local, mesh=mesh, in_specs=in_specs, out_specs=tokens, check_vma=False
    )
```

```python
import math

import jax
import jax.numpy as jnp
from jax import lax
from jax.experimental import pallas as pl
from jax.experimental.pallas import tpu as pltpu
from jax.sharding import PartitionSpec as P

HD = 128
QH = 12
STATE = 256
MI = 3072
EPSILON = 1e-05
NX = 4
NDP = 128
NY = 8
NZ = 8
TOK = 64
SPAN = 256
GW = 768
CACHED = 1024
FRESH = 128
MASK_LANE = 24
NEG = -1e30
LOG2E = 1.4426950408889634
SCALE = LOG2E / math.sqrt(HD)
MESH = pl.DeviceIdType.MESH
F32 = jnp.float32
BF16 = jnp.bfloat16
PARTS = 2
AUX, MAPS, XS, KV, Q, SCAN, ATT, LSE = 0, 1, 2, 3, 4, 5, 6, 6 + PARTS
KINDS = LSE + PARTS


def iota(shape, axis):
    return lax.broadcasted_iota(jnp.int32, shape, axis)


def level_of(device):
    z, y = device >> 4, (device >> 1) & 7
    return z - (z >> 2) * (z - 4) + (y >> 2)


LEVELS = [level_of(t) for t in range(NDP)]
TOP = 6
MEMBERS = [LEVELS.count(value) for value in range(TOP)]
EARLY = 4
SPLIT = sum(MEMBERS[:EARLY])


def dot_nt(a, b):
    return lax.dot_general(a, b, (((1,), (1,)), ((), ())), preferred_element_type=F32)


def dot_nn(a, b):
    return jnp.dot(a, b, preferred_element_type=F32)


def kernel(
    q, kv, xs, gate, maps, logit, mask, pool, page_map, length, prior, decay_log, step_bias,
    skip_gain, norm_gain, out,
    aux_own, aux_r, maps_r, xs_r, kv_r, q_r, pages, prior_v, gate_v, scan_s, scan_r, att_s, att_r,
    lse_s, lse_r, partial, keys, values, send_sem, recv_sem, page_send, page_recv, local_sem, early_sem,
    all_sem,
):
    d = lax.axis_index("dp")
    h = lax.axis_index("head")
    g, half = h // 2, h % 2
    level = level_of(d)
    side = (level >= EARLY).astype(jnp.int32)
    barrier = pltpu.get_barrier_semaphore()

    for k in range(1, NX):
        pl.semaphore_signal(barrier, 1, device_id=(d, (h + k) % NX), device_id_type=MESH)
    for t in sorted(range(NDP), key=lambda t: LEVELS[t]):

        @pl.when((level <= LEVELS[t]) & (d != t))
        def _():
            pl.semaphore_signal(barrier, 1, device_id=(t, h), device_id_type=MESH)

    greeted = NX - 1 - 1
    for value in range(TOP):
        greeted = greeted + jnp.where(level >= value, MEMBERS[value], 0)

    def group_cols(ref, index):
        return ref.at[:, pl.ds(pl.multiple_of(index * GW, 128), GW)]

    def fresh_part(index):
        return kv.at[
            pl.ds(pl.multiple_of((index % 2) * 32, 32), 32),
            pl.ds(pl.multiple_of((index // 2) * 256, 128), 256),
        ]

    locals_ = [
        pltpu.make_async_copy(maps, maps_r.at[h], local_sem.at[0]),
        pltpu.make_async_copy(group_cols(xs, h), xs_r.at[h], local_sem.at[1]),
        pltpu.make_async_copy(fresh_part(h), kv_r.at[h], local_sem.at[2]),
        pltpu.make_async_copy(group_cols(q, g), q_r.at[h], local_sem.at[3]),
        pltpu.make_async_copy(pool.at[d], pages.at[d], page_recv.at[side]),
        pltpu.make_async_copy(prior, prior_v, local_sem.at[4]),
        pltpu.make_async_copy(gate, gate_v, local_sem.at[5]),
    ]
    for copy in locals_:
        copy.start()

    eye = iota((TOK, TOK), 0) == iota((TOK, TOK), 1)
    own_mask = jnp.where(eye, jnp.broadcast_to(mask[...].astype(F32), (TOK, TOK)), 0.0)
    own_mask = jnp.sum((own_mask > 0.5).astype(F32), axis=1, keepdims=True)
    spread = (iota((24, 128), 0) == iota((24, 128), 1)).astype(BF16)
    aux = lax.dot_general(
        logit[...], spread, (((0,), (0,)), ((), ())), preferred_element_type=F32
    )
    aux = jnp.where(iota((TOK, 128), 1) == MASK_LANE, own_mask, aux).astype(BF16)
    aux_own[...] = aux
    aux_r[h] = aux

    pl.semaphore_wait(barrier, greeted)

    @pl.when(level == EARLY - 1)
    def _():
        for k in range(3):
            target = d - (SPLIT - 16) + 16 * k

            @pl.when(target < SPLIT - 16)
            def _():
                pl.semaphore_signal(early_sem, 1, device_id=(target, h), device_id_type=MESH)

    @pl.when(level == TOP - 1)
    def _():
        place = (((d - 64) >> 4) << 3) + (d & 7)
        for k in range(3):
            i = place + 32 * k
            target = jnp.where(i < 64, i, 64 + (((i - 64) >> 3) << 4) + (i & 7))
            pl.semaphore_signal(all_sem, 1, device_id=(target, h), device_id_type=MESH)


    def remote(kind, k, src, dst):
        return pltpu.make_async_remote_copy(
            src_ref=src,
            dst_ref=dst,
            send_sem=send_sem.at[kind, k],
            recv_sem=recv_sem.at[kind, k],
            device_id=(d, (h + k) % NX),
            device_id_type=MESH,
        )

    order = (1, 3, 2)
    sends = {}
    for k in order:
        sends[AUX, k] = remote(AUX, k, aux_own, aux_r.at[h])
    for k in order:
        sends[MAPS, k] = remote(MAPS, k, maps, maps_r.at[h])
    for k in order:
        sends[XS, k] = remote(XS, k, group_cols(xs, (h + k) % NX), xs_r.at[h])
    for k in order:
        sends[KV, k] = remote(KV, k, fresh_part((h + k) % NX), kv_r.at[h])
    for k in order:
        sends[Q, k] = remote(Q, k, group_cols(q, ((h + k) % NX) // 2), q_r.at[h])
    for copy in sends.values():
        copy.start()

    def send_pages(low, high):
        def step(i, carry):
            target = (d + i * 37) & (NDP - 1)
            other = level_of(target)

            @pl.when((other >= low) & (other <= high))
            def _():
                pltpu.make_async_remote_copy(
                    src_ref=pool.at[target],
                    dst_ref=pages.at[d],
                    send_sem=page_send,
                    recv_sem=page_recv.at[side],
                    device_id=(target, h),
                    device_id_type=MESH,
                ).start()

            return carry

        lax.fori_loop(1, NDP, step, 0)

    def settle(j):
        part = pl.ds(0, SPLIT if j == 0 else NDP - SPLIT)
        pltpu.make_async_copy(pool.at[part], pages.at[part], page_recv.at[j]).wait()

    send_pages(0, level)

    def arrive(kind):
        for k in order:
            sends[kind, k].wait_recv()

    @pl.when(level < EARLY - 1)
    def _():
        pl.semaphore_wait(early_sem, 1)
        send_pages(level + 1, EARLY - 1)

    @pl.when(level == EARLY)
    def _():
        pl.semaphore_wait(all_sem, 1)
        send_pages(TOP - 1, TOP - 1)


    @pl.when(level < EARLY)
    def _():
        pl.semaphore_wait(all_sem, 1)
        send_pages(EARLY, TOP - 1)

    arrive(AUX)
    aux_all = aux_r[...].reshape(SPAN, 128)
    rows, lanes = iota((128, 128), 0), iota((128, 128), 1)
    pick = ((rows == 6 * h + lanes) & (lanes < 6)).astype(BF16)
    own_logit = dot_nn(aux_all, pick)
    real = dot_nn(aux_all, (rows == MASK_LANE).astype(BF16))
    lane_row = iota((1, 128), 1)
    bias_row = jnp.zeros((1, 128), F32)
    rate_row = jnp.zeros((1, 128), F32)
    for j in range(6):
        bias_row = jnp.where(lane_row == j, step_bias[j], bias_row)
        rate_row = jnp.where(lane_row == j, decay_log[j], rate_row)
    rate_row = jnp.where(lane_row < 6, -jnp.exp(rate_row), 0.0)
    v = own_logit + bias_row
    steps = (jnp.maximum(v, 0.0) + jnp.log(1.0 + jnp.exp(-jnp.abs(v)))) * real
    log_decay = steps * rate_row
    causal = iota((SPAN, SPAN), 0) >= iota((SPAN, SPAN), 1)
    cumulative = jnp.dot(
        causal.astype(F32), log_decay, precision=lax.Precision.HIGHEST, preferred_element_type=F32
    )
    cumulative_t = cumulative.T
    steps_t = steps.T
    carry_weight = jnp.exp(cumulative)

    locals_[0].wait()
    locals_[5].wait()
    arrive(MAPS)
    in_map = maps_r[:, :, 0:STATE].reshape(SPAN, STATE)
    out_map = maps_r[:, :, STATE : 2 * STATE].reshape(SPAN, STATE)
    inter = dot_nt(out_map, in_map)
    locals_[1].wait()
    arrive(XS)
    for j in range(6):
        cols = pl.ds(j * HD, HD)
        gap = cumulative[:, j : j + 1] - cumulative_t[j : j + 1, :]
        weights = jnp.where(causal, jnp.exp(gap), 0.0) * inter * steps_t[j : j + 1, :]
        x = xs_r[:, :, cols].reshape(SPAN, HD)
        from_state = dot_nt(out_map, prior_v[pl.ds(j * HD, HD), :])
        result = dot_nn(weights.astype(BF16), x) + from_state * carry_weight[:, j : j + 1]
        result = (result + skip_gain[j] * x.astype(F32)) * real
        scan_s[:, :, cols] = result.astype(BF16).reshape(NX, TOK, HD)

    for k in order:
        sends[SCAN, k] = remote(SCAN, k, scan_s.at[(h + k) % NX], scan_r.at[h])
        sends[SCAN, k].start()


    one_hot = (page_map[...] == rows).astype(BF16)
    page_of = dot_nt(iota((8, 128), 1).astype(BF16), one_hot)
    expand = (iota((128, CACHED), 1) // 8 == iota((128, CACHED), 0)).astype(BF16)
    position = dot_nn(page_of.astype(BF16), expand)[0:1, :] * 16.0
    position = position + (half * 8 + iota((1, CACHED), 1) % 8).astype(F32)
    cache_bias = jnp.where(position < length[...].astype(F32), 0.0, NEG)
    slot_row = dot_nt((iota((8, 128), 1) == MASK_LANE).astype(BF16), aux_all)

    def slot_of(key):
        return (key // 32) * TOK + half * 32 + key % 32

    pick_slot = (iota((SPAN, FRESH), 0) == slot_of(iota((SPAN, FRESH), 1))).astype(BF16)
    real_row = dot_nn(slot_row.astype(BF16), pick_slot)[0:1, :]
    seen = (slot_of(iota((SPAN, FRESH), 1)) <= iota((SPAN, FRESH), 0)) & (real_row > 0.5)
    fresh_bias = jnp.where(seen, 0.0, NEG)

    first, last = pl.ds(0, 8 * SPLIT), pl.ds(8 * SPLIT, CACHED + FRESH - 8 * SPLIT)
    first_bias = cache_bias[:, 0 : 8 * SPLIT]
    last_bias = jnp.concatenate(
        [jnp.broadcast_to(cache_bias[:, 8 * SPLIT : CACHED], (SPAN, CACHED - 8 * SPLIT)), fresh_bias],
        axis=1,
    )
    locals_[2].wait()
    locals_[3].wait()
    arrive(KV)
    keys[pl.ds(CACHED, FRESH), :] = kv_r[:, :, 0:HD].reshape(FRESH, HD)
    values[pl.ds(CACHED, FRESH), :] = kv_r[:, :, HD : 2 * HD].reshape(FRESH, HD)
    arrive(Q)
    settle(0)
    keys[first, :] = pages[0:SPLIT, :, 0:HD].reshape(8 * SPLIT, HD)
    values[first, :] = pages[0:SPLIT, :, HD : 2 * HD].reshape(8 * SPLIT, HD)
    tops, totals = [], []
    for j in range(6):
        query = q_r[:, :, pl.ds(j * HD, HD)].reshape(SPAN, HD)
        scores = dot_nt(query, keys[first, :]) + first_bias
        top = jnp.max(scores, axis=1, keepdims=True)
        terms = jnp.exp2((scores - top) * SCALE)
        tops.append(top)
        totals.append(jnp.sum(terms, axis=1, keepdims=True))
        partial[j] = dot_nn(terms.astype(BF16), values[first, :])

    settle(1)
    rest = pl.ds(8 * SPLIT, CACHED - 8 * SPLIT)
    keys[rest, :] = pages[SPLIT:NDP, :, 0:HD].reshape(CACHED - 8 * SPLIT, HD)
    values[rest, :] = pages[SPLIT:NDP, :, HD : 2 * HD].reshape(CACHED - 8 * SPLIT, HD)
    per = 6 // PARTS
    for part in range(PARTS):
        lse = jnp.zeros((SPAN, 128), F32)
        for j in range(part * per, (part + 1) * per):
            cols = pl.ds(j * HD, HD)
            query = q_r[:, :, cols].reshape(SPAN, HD)
            scores = dot_nt(query, keys[last, :]) + last_bias
            top = jnp.maximum(tops[j], jnp.max(scores, axis=1, keepdims=True))
            terms = jnp.exp2((scores - top) * SCALE)
            before = jnp.exp2((tops[j] - top) * SCALE)
            total = totals[j] * before + jnp.sum(terms, axis=1, keepdims=True)
            weighted = partial[j] * before + dot_nn(terms.astype(BF16), values[last, :])
            att_s[:, :, cols] = (weighted / total).astype(BF16).reshape(NX, TOK, HD)
            lse = jnp.where(
                iota((SPAN, 128), 1) == j - part * per, top * SCALE + jnp.log2(total), lse
            )
        for u in range(NX):
            lse_s[part, u] = lse[u * TOK : (u + 1) * TOK, :].T[0:8, :]
        width = pl.ds(part * per * HD, per * HD)
        for k in order:
            to = (h + k) % NX
            sends[LSE + part, k] = remote(LSE + part, k, lse_s.at[part, to], lse_r.at[part, h])
            sends[LSE + part, k].start()
            sends[ATT + part, k] = remote(
                ATT + part, k, att_s.at[to, :, width], att_r.at[h, :, width]
            )
            sends[ATT + part, k].start()

    locals_[6].wait()
    scan_r[h] = scan_s[h]
    arrive(SCAN)
    squares = jnp.zeros((TOK, 1), F32)
    for u in range(NX):
        z_in = gate_v[:, pl.ds(u * GW, GW)].astype(F32)
        gated = scan_r[u].astype(F32) * (z_in / (1.0 + jnp.exp(-z_in)))
        squares = squares + jnp.sum(gated * gated, axis=1, keepdims=True)
    inverse = lax.rsqrt(squares / MI + EPSILON)
    for u in range(NX):
        z_in = gate_v[:, pl.ds(u * GW, GW)].astype(F32)
        gated = scan_r[u].astype(F32) * (z_in / (1.0 + jnp.exp(-z_in)))
        normed = gated * inverse * norm_gain[:, pl.ds(u * GW, GW)]
        out[:, pl.ds(QH * HD + u * GW, GW)] = normed.astype(BF16)

    att_r[h] = att_s[h]
    for part in range(PARTS):
        lse_r[part, h] = lse_s[part, h]
        arrive(LSE + part)
        arrive(ATT + part)
        lse_all = lse_r[part].reshape(32, TOK).T
        for group in range(2):
            a, b = 2 * group, 2 * group + 1
            for i in range(per):
                one = lse_all[:, a * 8 + i : a * 8 + i + 1]
                two = lse_all[:, b * 8 + i : b * 8 + i + 1]
                cols = pl.ds((part * per + i) * HD, HD)
                joined = att_r[a, :, cols].astype(F32) * (own_mask / (1.0 + jnp.exp2(two - one)))
                joined = joined + att_r[b, :, cols].astype(F32) * (
                    own_mask / (1.0 + jnp.exp2(one - two))
                )
                out[:, pl.ds(group * GW + (part * per + i) * HD, HD)] = joined.astype(BF16)

    for copy in sends.values():
        copy.wait_send()
    pltpu.make_async_remote_copy(
        src_ref=pool.at[pl.ds(0, NDP - 1)],
        dst_ref=pages.at[pl.ds(0, NDP - 1)],
        send_sem=page_send,
        recv_sem=page_recv.at[0],
        device_id=(d, (h + 1) % NX),
        device_id_type=MESH,
    ).wait_send()


def local(
    queries, fresh_keyvals, ssm_input, gate_input, state_maps, step_logit, slot_mask, cache_pool,
    page_map, cached_lengths, prior_state, decay_log, step_bias, skip_gain, norm_gain,
):
    hbm = pl.BlockSpec(memory_space=pl.ANY)
    vmem = pl.BlockSpec(memory_space=pltpu.VMEM)
    smem = pl.BlockSpec(memory_space=pltpu.SMEM)
    return pl.pallas_call(
        kernel,
        out_shape=jax.ShapeDtypeStruct((TOK, QH * HD + MI), BF16),
        in_specs=[
            hbm, hbm, hbm, hbm, hbm, vmem, vmem, hbm, vmem, vmem, hbm, smem, smem, smem, vmem,
        ],
        out_specs=vmem,
        scratch_shapes=[
            pltpu.VMEM((TOK, 128), BF16),
            pltpu.VMEM((NX, TOK, 128), BF16),
            pltpu.VMEM((NX, TOK, 2 * STATE), BF16),
            pltpu.VMEM((NX, TOK, GW), BF16),
            pltpu.VMEM((NX, 32, 2 * HD), BF16),
            pltpu.VMEM((NX, TOK, GW), BF16),
            pltpu.VMEM((NDP, 8, 2 * HD), BF16),
            pltpu.VMEM((GW, STATE), BF16),
            pltpu.VMEM((TOK, MI), BF16),
            pltpu.VMEM((NX, TOK, GW), BF16),
            pltpu.VMEM((NX, TOK, GW), BF16),
            pltpu.VMEM((NX, TOK, GW), BF16),
            pltpu.VMEM((NX, TOK, GW), BF16),
            pltpu.VMEM((PARTS, NX, 8, TOK), F32),
            pltpu.VMEM((PARTS, NX, 8, TOK), F32),
            pltpu.VMEM((6, SPAN, HD), F32),
            pltpu.VMEM((CACHED + FRESH, HD), BF16),
            pltpu.VMEM((CACHED + FRESH, HD), BF16),
            pltpu.SemaphoreType.DMA((KINDS, NX)),
            pltpu.SemaphoreType.DMA((KINDS, NX)),
            pltpu.SemaphoreType.DMA,
            pltpu.SemaphoreType.DMA((2,)),
            pltpu.SemaphoreType.DMA((6,)),
            pltpu.SemaphoreType.REGULAR,
            pltpu.SemaphoreType.REGULAR,
        ],
        compiler_params=pltpu.CompilerParams(collective_id=0, has_side_effects=True),
        name="mixer",
    )(
        queries, fresh_keyvals, ssm_input, gate_input, state_maps, step_logit.T,
        slot_mask.reshape(1, TOK), cache_pool, page_map, cached_lengths.reshape(1, 1),
        prior_state.reshape(GW, STATE), decay_log, step_bias, skip_gain, norm_gain.reshape(1, MI),
    )


def solution(mesh):
    tokens = P(("dp", "head"), None)
    in_specs = (
        tokens, tokens, tokens, tokens, tokens, tokens,
        P(("dp", "head")),
        P("dp", "head", None),
        P("dp", None),
        P("dp"),
        P("dp", "head", None, None),
        P("head"), P("head"), P("head"),
        P(),
    )
    return jax.shard_map(
        local, mesh=mesh, in_specs=in_specs, out_specs=tokens, check_vma=False
    )
```

```python
import math

import jax
import jax.numpy as jnp
from jax import lax
from jax.experimental import pallas as pl
from jax.experimental.pallas import tpu as pltpu
from jax.sharding import PartitionSpec as P

HD = 128
QH = 12
STATE = 256
MI = 3072
EPSILON = 1e-05
NX = 4
NDP = 128
NY = 8
NZ = 8
TOK = 64
SPAN = 256
GW = 768
CACHED = 1024
FRESH = 128
MASK_LANE = 24
NEG = -1e30
LOG2E = 1.4426950408889634
SCALE = LOG2E / math.sqrt(HD)
MESH = pl.DeviceIdType.MESH
F32 = jnp.float32
BF16 = jnp.bfloat16
PARTS = 2
AUX, MAPS, XS, KV, Q, SCAN, ATT, LSE = 0, 1, 2, 3, 4, 5, 6, 6 + PARTS
KINDS = LSE + PARTS


def iota(shape, axis):
    return lax.broadcasted_iota(jnp.int32, shape, axis)


def level_of(device):
    z, y = device >> 4, (device >> 1) & 7
    return z + (y >> 2) + (z >> 2) * (1 + 3 * (y >> 2)) + 2 * (device < 1)


LEVELS = [level_of(t) for t in range(NDP)]
TOP = 13
MEMBERS = [LEVELS.count(value) for value in range(TOP)]
EARLY = 5
SPLIT = sum(MEMBERS[:EARLY])


def dot_nt(a, b):
    return lax.dot_general(a, b, (((1,), (1,)), ((), ())), preferred_element_type=F32)


def dot_nn(a, b):
    return jnp.dot(a, b, preferred_element_type=F32)


def kernel(
    q, kv, xs, gate, maps, logit, mask, pool, page_map, length, prior, decay_log, step_bias,
    skip_gain, norm_gain, out,
    aux_own, aux_r, maps_r, xs_r, kv_r, q_r, pages, prior_v, gate_v, scan_s, scan_r, att_s, att_r,
    lse_s, lse_r, partial, keys, values, send_sem, recv_sem, page_send, page_recv, local_sem, early_sem,
    all_sem,
):
    d = lax.axis_index("dp")
    h = lax.axis_index("head")
    g, half = h // 2, h % 2
    level = level_of(d)
    side = (level >= EARLY).astype(jnp.int32)
    barrier = pltpu.get_barrier_semaphore()

    for k in range(1, NX):
        pl.semaphore_signal(barrier, 1, device_id=(d, (h + k) % NX), device_id_type=MESH)
    for t in sorted(range(NDP), key=lambda t: LEVELS[t]):

        @pl.when((level <= LEVELS[t]) & (d != t))
        def _():
            pl.semaphore_signal(barrier, 1, device_id=(t, h), device_id_type=MESH)

    greeted = NX - 1 - 1
    for value in range(TOP):
        greeted = greeted + jnp.where(level >= value, MEMBERS[value], 0)

    def group_cols(ref, index):
        return ref.at[:, pl.ds(pl.multiple_of(index * GW, 128), GW)]

    def fresh_part(index):
        return kv.at[
            pl.ds(pl.multiple_of((index % 2) * 32, 32), 32),
            pl.ds(pl.multiple_of((index // 2) * 256, 128), 256),
        ]

    locals_ = [
        pltpu.make_async_copy(maps, maps_r.at[h], local_sem.at[0]),
        pltpu.make_async_copy(group_cols(xs, h), xs_r.at[h], local_sem.at[1]),
        pltpu.make_async_copy(fresh_part(h), kv_r.at[h], local_sem.at[2]),
        pltpu.make_async_copy(group_cols(q, g), q_r.at[h], local_sem.at[3]),
        pltpu.make_async_copy(pool.at[d], pages.at[d], page_recv.at[side]),
        pltpu.make_async_copy(prior, prior_v, local_sem.at[4]),
        pltpu.make_async_copy(gate, gate_v, local_sem.at[5]),
    ]
    for copy in locals_:
        copy.start()

    eye = iota((TOK, TOK), 0) == iota((TOK, TOK), 1)
    own_mask = jnp.where(eye, jnp.broadcast_to(mask[...].astype(F32), (TOK, TOK)), 0.0)
    own_mask = jnp.sum((own_mask > 0.5).astype(F32), axis=1, keepdims=True)
    spread = (iota((24, 128), 0) == iota((24, 128), 1)).astype(BF16)
    aux = lax.dot_general(
        logit[...], spread, (((0,), (0,)), ((), ())), preferred_element_type=F32
    )
    aux = jnp.where(iota((TOK, 128), 1) == MASK_LANE, own_mask, aux).astype(BF16)
    aux_own[...] = aux
    aux_r[h] = aux

    pl.semaphore_wait(barrier, greeted)

    @pl.when(level == EARLY - 1)
    def _():
        for k in range(7):
            target = d - 56 + 8 * k
            pl.semaphore_signal(early_sem, 1, device_id=(target, h), device_id_type=MESH)

    @pl.when(level == TOP - 1)
    def _():
        for k in range(15):
            target = d - 120 + 8 * k
            pl.semaphore_signal(all_sem, 1, device_id=(target, h), device_id_type=MESH)

    def remote(kind, k, src, dst):
        return pltpu.make_async_remote_copy(
            src_ref=src,
            dst_ref=dst,
            send_sem=send_sem.at[kind, k],
            recv_sem=recv_sem.at[kind, k],
            device_id=(d, (h + k) % NX),
            device_id_type=MESH,
        )

    order = (2, 1, 3)
    sends = {}
    for k in order:
        sends[AUX, k] = remote(AUX, k, aux_own, aux_r.at[h])
    for k in order:
        sends[MAPS, k] = remote(MAPS, k, maps, maps_r.at[h])
    for k in order:
        sends[XS, k] = remote(XS, k, group_cols(xs, (h + k) % NX), xs_r.at[h])
    for k in order:
        sends[KV, k] = remote(KV, k, fresh_part((h + k) % NX), kv_r.at[h])
    for k in order:
        sends[Q, k] = remote(Q, k, group_cols(q, ((h + k) % NX) // 2), q_r.at[h])
    for copy in sends.values():
        copy.start()

    def send_pages(low, high):
        def step(i, carry):
            target = (d + i * 45) & (NDP - 1)
            other = level_of(target)

            @pl.when((other >= low) & (other <= high))
            def _():
                pltpu.make_async_remote_copy(
                    src_ref=pool.at[target],
                    dst_ref=pages.at[d],
                    send_sem=page_send,
                    recv_sem=page_recv.at[side],
                    device_id=(target, h),
                    device_id_type=MESH,
                ).start()

            return carry

        lax.fori_loop(1, NDP, step, 0)

    def settle(j):
        part = pl.ds(0, SPLIT if j == 0 else NDP - SPLIT)
        pltpu.make_async_copy(pool.at[part], pages.at[part], page_recv.at[j]).wait()

    send_pages(0, jnp.minimum(level, EARLY - 1))

    @pl.when(level >= EARLY)
    def _():
        send_pages(EARLY, level)


    def arrive(kind):
        for k in order:
            sends[kind, k].wait_recv()

    @pl.when(level < EARLY - 1)
    def _():
        pl.semaphore_wait(early_sem, 1)
        send_pages(level + 1, EARLY - 1)

    @pl.when((level >= EARLY) & (level < TOP - 1))
    def _():
        pl.semaphore_wait(all_sem, 1)
        send_pages(level + 1, TOP - 1)


    @pl.when(level < EARLY)
    def _():
        pl.semaphore_wait(all_sem, 1)
        send_pages(EARLY, TOP - 1)

    arrive(AUX)
    aux_all = aux_r[...].reshape(SPAN, 128)
    rows, lanes = iota((128, 128), 0), iota((128, 128), 1)
    pick = ((rows == 6 * h + lanes) & (lanes < 6)).astype(BF16)
    own_logit = dot_nn(aux_all, pick)
    real = dot_nn(aux_all, (rows == MASK_LANE).astype(BF16))
    lane_row = iota((1, 128), 1)
    bias_row = jnp.zeros((1, 128), F32)
    rate_row = jnp.zeros((1, 128), F32)
    for j in range(6):
        bias_row = jnp.where(lane_row == j, step_bias[j], bias_row)
        rate_row = jnp.where(lane_row == j, decay_log[j], rate_row)
    rate_row = jnp.where(lane_row < 6, -jnp.exp(rate_row), 0.0)
    v = own_logit + bias_row
    steps = (jnp.maximum(v, 0.0) + jnp.log(1.0 + jnp.exp(-jnp.abs(v)))) * real
    log_decay = steps * rate_row
    causal = iota((SPAN, SPAN), 0) >= iota((SPAN, SPAN), 1)
    cumulative = jnp.dot(
        causal.astype(F32), log_decay, precision=lax.Precision.HIGHEST, preferred_element_type=F32
    )
    cumulative_t = cumulative.T
    steps_t = steps.T
    carry_weight = jnp.exp(cumulative)

    locals_[0].wait()
    locals_[5].wait()
    arrive(MAPS)
    in_map = maps_r[:, :, 0:STATE].reshape(SPAN, STATE)
    out_map = maps_r[:, :, STATE : 2 * STATE].reshape(SPAN, STATE)
    inter = dot_nt(out_map, in_map)
    locals_[1].wait()
    arrive(XS)
    for j in range(6):
        cols = pl.ds(j * HD, HD)
        gap = cumulative[:, j : j + 1] - cumulative_t[j : j + 1, :]
        weights = jnp.where(causal, jnp.exp(gap), 0.0) * inter * steps_t[j : j + 1, :]
        x = xs_r[:, :, cols].reshape(SPAN, HD)
        from_state = dot_nt(out_map, prior_v[pl.ds(j * HD, HD), :])
        result = dot_nn(weights.astype(BF16), x) + from_state * carry_weight[:, j : j + 1]
        result = (result + skip_gain[j] * x.astype(F32)) * real
        scan_s[:, :, cols] = result.astype(BF16).reshape(NX, TOK, HD)

    for k in order:
        sends[SCAN, k] = remote(SCAN, k, scan_s.at[(h + k) % NX], scan_r.at[h])
        sends[SCAN, k].start()


    one_hot = (page_map[...] == rows).astype(BF16)
    page_of = dot_nt(iota((8, 128), 1).astype(BF16), one_hot)
    expand = (iota((128, CACHED), 1) // 8 == iota((128, CACHED), 0)).astype(BF16)
    position = dot_nn(page_of.astype(BF16), expand)[0:1, :] * 16.0
    position = position + (half * 8 + iota((1, CACHED), 1) % 8).astype(F32)
    cache_bias = jnp.where(position < length[...].astype(F32), 0.0, NEG)
    slot_row = dot_nt((iota((8, 128), 1) == MASK_LANE).astype(BF16), aux_all)

    def slot_of(key):
        return (key // 32) * TOK + half * 32 + key % 32

    pick_slot = (iota((SPAN, FRESH), 0) == slot_of(iota((SPAN, FRESH), 1))).astype(BF16)
    real_row = dot_nn(slot_row.astype(BF16), pick_slot)[0:1, :]
    seen = (slot_of(iota((SPAN, FRESH), 1)) <= iota((SPAN, FRESH), 0)) & (real_row > 0.5)
    fresh_bias = jnp.where(seen, 0.0, NEG)

    near = FRESH + 8 * SPLIT
    first, last = pl.ds(0, near), pl.ds(near, CACHED + FRESH - near)
    first_bias = jnp.concatenate(
        [fresh_bias, jnp.broadcast_to(cache_bias[:, 0 : 8 * SPLIT], (SPAN, 8 * SPLIT))], axis=1
    )
    last_bias = cache_bias[:, 8 * SPLIT : CACHED]
    locals_[2].wait()
    locals_[3].wait()
    arrive(KV)
    keys[pl.ds(0, FRESH), :] = kv_r[:, :, 0:HD].reshape(FRESH, HD)
    values[pl.ds(0, FRESH), :] = kv_r[:, :, HD : 2 * HD].reshape(FRESH, HD)
    arrive(Q)
    settle(0)
    keys[pl.ds(FRESH, 8 * SPLIT), :] = pages[0:SPLIT, :, 0:HD].reshape(8 * SPLIT, HD)
    values[pl.ds(FRESH, 8 * SPLIT), :] = pages[0:SPLIT, :, HD : 2 * HD].reshape(8 * SPLIT, HD)
    tops, totals = [], []
    for j in range(6):
        query = q_r[:, :, pl.ds(j * HD, HD)].reshape(SPAN, HD)
        scores = dot_nt(query, keys[first, :]) + first_bias
        top = jnp.max(scores, axis=1, keepdims=True)
        terms = jnp.exp2((scores - top) * SCALE)
        tops.append(top)
        totals.append(jnp.sum(terms, axis=1, keepdims=True))
        partial[j] = dot_nn(terms.astype(BF16), values[first, :])

    settle(1)
    keys[last, :] = pages[SPLIT:NDP, :, 0:HD].reshape(CACHED - 8 * SPLIT, HD)
    values[last, :] = pages[SPLIT:NDP, :, HD : 2 * HD].reshape(CACHED - 8 * SPLIT, HD)
    per = 6 // PARTS
    for part in range(PARTS):
        lse = jnp.zeros((SPAN, 128), F32)
        for j in range(part * per, (part + 1) * per):
            cols = pl.ds(j * HD, HD)
            query = q_r[:, :, cols].reshape(SPAN, HD)
            scores = dot_nt(query, keys[last, :]) + last_bias
            top = jnp.maximum(tops[j], jnp.max(scores, axis=1, keepdims=True))
            terms = jnp.exp2((scores - top) * SCALE)
            before = jnp.exp2((tops[j] - top) * SCALE)
            total = totals[j] * before + jnp.sum(terms, axis=1, keepdims=True)
            weighted = partial[j] * before + dot_nn(terms.astype(BF16), values[last, :])
            att_s[:, :, cols] = (weighted / total).astype(BF16).reshape(NX, TOK, HD)
            lse = jnp.where(
                iota((SPAN, 128), 1) == j - part * per, top * SCALE + jnp.log2(total), lse
            )
        for u in range(NX):
            lse_s[part, u] = lse[u * TOK : (u + 1) * TOK, :].T[0:8, :]
        width = pl.ds(part * per * HD, per * HD)
        for k in order:
            to = (h + k) % NX
            sends[LSE + part, k] = remote(LSE + part, k, lse_s.at[part, to], lse_r.at[part, h])
            sends[LSE + part, k].start()
            sends[ATT + part, k] = remote(
                ATT + part, k, att_s.at[to, :, width], att_r.at[h, :, width]
            )
            sends[ATT + part, k].start()

    locals_[6].wait()
    scan_r[h] = scan_s[h]
    arrive(SCAN)
    squares = jnp.zeros((TOK, 1), F32)
    for u in range(NX):
        z_in = gate_v[:, pl.ds(u * GW, GW)].astype(F32)
        gated = scan_r[u].astype(F32) * (z_in / (1.0 + jnp.exp(-z_in)))
        squares = squares + jnp.sum(gated * gated, axis=1, keepdims=True)
    inverse = lax.rsqrt(squares / MI + EPSILON)
    for u in range(NX):
        z_in = gate_v[:, pl.ds(u * GW, GW)].astype(F32)
        gated = scan_r[u].astype(F32) * (z_in / (1.0 + jnp.exp(-z_in)))
        normed = gated * inverse * norm_gain[:, pl.ds(u * GW, GW)]
        out[:, pl.ds(QH * HD + u * GW, GW)] = normed.astype(BF16)

    att_r[h] = att_s[h]
    for part in range(PARTS):
        lse_r[part, h] = lse_s[part, h]
        arrive(LSE + part)
        arrive(ATT + part)
        lse_all = lse_r[part].reshape(32, TOK).T
        for group in range(2):
            a, b = 2 * group, 2 * group + 1
            for i in range(per):
                one = lse_all[:, a * 8 + i : a * 8 + i + 1]
                two = lse_all[:, b * 8 + i : b * 8 + i + 1]
                cols = pl.ds((part * per + i) * HD, HD)
                joined = att_r[a, :, cols].astype(F32) * (own_mask / (1.0 + jnp.exp2(two - one)))
                joined = joined + att_r[b, :, cols].astype(F32) * (
                    own_mask / (1.0 + jnp.exp2(one - two))
                )
                out[:, pl.ds(group * GW + (part * per + i) * HD, HD)] = joined.astype(BF16)

    for copy in sends.values():
        copy.wait_send()
    pltpu.make_async_remote_copy(
        src_ref=pool.at[pl.ds(0, NDP - 1)],
        dst_ref=pages.at[pl.ds(0, NDP - 1)],
        send_sem=page_send,
        recv_sem=page_recv.at[0],
        device_id=(d, (h + 1) % NX),
        device_id_type=MESH,
    ).wait_send()


def local(
    queries, fresh_keyvals, ssm_input, gate_input, state_maps, step_logit, slot_mask, cache_pool,
    page_map, cached_lengths, prior_state, decay_log, step_bias, skip_gain, norm_gain,
):
    hbm = pl.BlockSpec(memory_space=pl.ANY)
    vmem = pl.BlockSpec(memory_space=pltpu.VMEM)
    smem = pl.BlockSpec(memory_space=pltpu.SMEM)
    return pl.pallas_call(
        kernel,
        out_shape=pltpu.VMEM((TOK, QH * HD + MI), BF16),
        in_specs=[
            hbm, hbm, hbm, hbm, hbm, vmem, vmem, hbm, vmem, vmem, hbm, smem, smem, smem, vmem,
        ],
        out_specs=vmem,
        scratch_shapes=[
            pltpu.VMEM((TOK, 128), BF16),
            pltpu.VMEM((NX, TOK, 128), BF16),
            pltpu.VMEM((NX, TOK, 2 * STATE), BF16),
            pltpu.VMEM((NX, TOK, GW), BF16),
            pltpu.VMEM((NX, 32, 2 * HD), BF16),
            pltpu.VMEM((NX, TOK, GW), BF16),
            pltpu.VMEM((NDP, 8, 2 * HD), BF16),
            pltpu.VMEM((GW, STATE), BF16),
            pltpu.VMEM((TOK, MI), BF16),
            pltpu.VMEM((NX, TOK, GW), BF16),
            pltpu.VMEM((NX, TOK, GW), BF16),
            pltpu.VMEM((NX, TOK, GW), BF16),
            pltpu.VMEM((NX, TOK, GW), BF16),
            pltpu.VMEM((PARTS, NX, 8, TOK), F32),
            pltpu.VMEM((PARTS, NX, 8, TOK), F32),
            pltpu.VMEM((6, SPAN, HD), F32),
            pltpu.VMEM((CACHED + FRESH, HD), BF16),
            pltpu.VMEM((CACHED + FRESH, HD), BF16),
            pltpu.SemaphoreType.DMA((KINDS, NX)),
            pltpu.SemaphoreType.DMA((KINDS, NX)),
            pltpu.SemaphoreType.DMA,
            pltpu.SemaphoreType.DMA((2,)),
            pltpu.SemaphoreType.DMA((6,)),
            pltpu.SemaphoreType.REGULAR,
            pltpu.SemaphoreType.REGULAR,
        ],
        compiler_params=pltpu.CompilerParams(collective_id=0, has_side_effects=True),
        name="mixer",
    )(
        queries, fresh_keyvals, ssm_input, gate_input, state_maps, step_logit.T,
        slot_mask.reshape(1, TOK), cache_pool, page_map, cached_lengths.reshape(1, 1),
        prior_state.reshape(GW, STATE), decay_log, step_bias, skip_gain, norm_gain.reshape(1, MI),
    )


def solution(mesh):
    tokens = P(("dp", "head"), None)
    in_specs = (
        tokens, tokens, tokens, tokens, tokens, tokens,
        P(("dp", "head")),
        P("dp", "head", None),
        P("dp", None),
        P("dp"),
        P("dp", "head", None, None),
        P("head"), P("head"), P("head"),
        P(),
    )
    return jax.shard_map(
        local, mesh=mesh, in_specs=in_specs, out_specs=tokens, check_vma=False
    )
```

```python
import math

import jax
import jax.numpy as jnp
from jax import lax
from jax.experimental import pallas as pl
from jax.experimental.pallas import tpu as pltpu
from jax.sharding import PartitionSpec as P

HD = 128
QH = 12
STATE = 256
MI = 3072
EPSILON = 1e-05
NX = 4
NDP = 128
NY = 8
NZ = 8
TOK = 64
SPAN = 256
GW = 768
CACHED = 1024
FRESH = 128
MASK_LANE = 24
NEG = -1e30
LOG2E = 1.4426950408889634
SCALE = LOG2E / math.sqrt(HD)
MESH = pl.DeviceIdType.MESH
F32 = jnp.float32
BF16 = jnp.bfloat16
PARTS = 3
AUX, MAPS, XS, KV, Q, SCAN, ATT, LSE = 0, 1, 2, 3, 4, 5, 6, 6 + PARTS
KINDS = LSE + PARTS


def iota(shape, axis):
    return lax.broadcasted_iota(jnp.int32, shape, axis)


def level_of(device):
    z, y = device >> 4, (device >> 1) & 7
    return z + (y >> 2) + (z >> 2) * (1 + 3 * (y >> 2)) + 2 * (device < 1)


LEVELS = [level_of(t) for t in range(NDP)]
TOP = 13
MEMBERS = [LEVELS.count(value) for value in range(TOP)]
EARLY = 5
SPLIT = sum(MEMBERS[:EARLY])


def dot_nt(a, b):
    return lax.dot_general(a, b, (((1,), (1,)), ((), ())), preferred_element_type=F32)


def dot_nn(a, b):
    return jnp.dot(a, b, preferred_element_type=F32)


def kernel(
    q, kv, xs, gate, maps, logit, mask, pool, page_map, length, prior, decay_log, step_bias,
    skip_gain, norm_gain, out,
    aux_own, aux_r, maps_r, xs_r, kv_r, q_r, pages, prior_v, gate_v, scan_s, scan_r, att_s, att_r,
    lse_s, lse_r, partial, keys, values, send_sem, recv_sem, page_send, page_recv, local_sem, early_sem,
    all_sem,
):
    d = lax.axis_index("dp")
    h = lax.axis_index("head")
    g, half = h // 2, h % 2
    level = level_of(d)
    side = (level >= EARLY).astype(jnp.int32)
    barrier = pltpu.get_barrier_semaphore()

    for k in range(1, NX):
        pl.semaphore_signal(barrier, 1, device_id=(d, (h + k) % NX), device_id_type=MESH)
    for t in sorted(range(NDP), key=lambda t: LEVELS[t]):

        @pl.when((level <= LEVELS[t]) & (d != t))
        def _():
            pl.semaphore_signal(barrier, 1, device_id=(t, h), device_id_type=MESH)

    greeted = NX - 1 - 1
    for value in range(TOP):
        greeted = greeted + jnp.where(level >= value, MEMBERS[value], 0)

    def group_cols(ref, index):
        return ref.at[:, pl.ds(pl.multiple_of(index * GW, 128), GW)]

    def fresh_part(index):
        return kv.at[
            pl.ds(pl.multiple_of((index % 2) * 32, 32), 32),
            pl.ds(pl.multiple_of((index // 2) * 256, 128), 256),
        ]

    locals_ = [
        pltpu.make_async_copy(maps, maps_r.at[h], local_sem.at[0]),
        pltpu.make_async_copy(group_cols(xs, h), xs_r.at[h], local_sem.at[1]),
        pltpu.make_async_copy(fresh_part(h), kv_r.at[h], local_sem.at[2]),
        pltpu.make_async_copy(group_cols(q, g), q_r.at[h], local_sem.at[3]),
        pltpu.make_async_copy(pool.at[d], pages.at[d], page_recv.at[side]),
        pltpu.make_async_copy(prior, prior_v, local_sem.at[4]),
        pltpu.make_async_copy(gate, gate_v, local_sem.at[5]),
    ]
    for copy in locals_:
        copy.start()

    eye = iota((TOK, TOK), 0) == iota((TOK, TOK), 1)
    own_mask = jnp.where(eye, jnp.broadcast_to(mask[...].astype(F32), (TOK, TOK)), 0.0)
    own_mask = jnp.sum((own_mask > 0.5).astype(F32), axis=1, keepdims=True)
    spread = (iota((24, 128), 0) == iota((24, 128), 1)).astype(BF16)
    aux = lax.dot_general(
        logit[...], spread, (((0,), (0,)), ((), ())), preferred_element_type=F32
    )
    aux = jnp.where(iota((TOK, 128), 1) == MASK_LANE, own_mask, aux).astype(BF16)
    aux_own[...] = aux
    aux_r[h] = aux

    pl.semaphore_wait(barrier, greeted)

    @pl.when(level == EARLY - 1)
    def _():
        for k in range(7):
            target = d - 56 + 8 * k
            pl.semaphore_signal(early_sem, 1, device_id=(target, h), device_id_type=MESH)

    @pl.when(level == TOP - 1)
    def _():
        for k in range(15):
            target = d - 120 + 8 * k
            pl.semaphore_signal(all_sem, 1, device_id=(target, h), device_id_type=MESH)

    def remote(kind, k, src, dst):
        return pltpu.make_async_remote_copy(
            src_ref=src,
            dst_ref=dst,
            send_sem=send_sem.at[kind, k],
            recv_sem=recv_sem.at[kind, k],
            device_id=(d, (h + k) % NX),
            device_id_type=MESH,
        )

    order = (2, 1, 3)
    sends = {}
    for k in order:
        sends[AUX, k] = remote(AUX, k, aux_own, aux_r.at[h])
    for k in order:
        sends[MAPS, k] = remote(MAPS, k, maps, maps_r.at[h])
    for k in order:
        sends[XS, k] = remote(XS, k, group_cols(xs, (h + k) % NX), xs_r.at[h])
    for k in order:
        sends[KV, k] = remote(KV, k, fresh_part((h + k) % NX), kv_r.at[h])
    for k in order:
        sends[Q, k] = remote(Q, k, group_cols(q, ((h + k) % NX) // 2), q_r.at[h])
    for copy in sends.values():
        copy.start()

    def send_pages(low, high):
        def step(i, carry):
            target = (d + i * 45) & (NDP - 1)
            other = level_of(target)

            @pl.when((other >= low) & (other <= high))
            def _():
                pltpu.make_async_remote_copy(
                    src_ref=pool.at[target],
                    dst_ref=pages.at[d],
                    send_sem=page_send,
                    recv_sem=page_recv.at[side],
                    device_id=(target, h),
                    device_id_type=MESH,
                ).start()

            return carry

        lax.fori_loop(1, NDP, step, 0)

    def settle(j):
        part = pl.ds(0, SPLIT if j == 0 else NDP - SPLIT)
        pltpu.make_async_copy(pool.at[part], pages.at[part], page_recv.at[j]).wait()

    send_pages(0, jnp.minimum(level, 1))

    @pl.when(level >= 2)
    def _():
        send_pages(2, jnp.minimum(level, EARLY - 1))


    @pl.when(level >= EARLY)
    def _():
        send_pages(EARLY, level)


    def arrive(kind):
        for k in order:
            sends[kind, k].wait_recv()

    @pl.when(level < EARLY - 1)
    def _():
        pl.semaphore_wait(early_sem, 1)
        send_pages(level + 1, EARLY - 1)

    @pl.when((level >= EARLY) & (level < TOP - 1))
    def _():
        pl.semaphore_wait(all_sem, 1)
        send_pages(level + 1, TOP - 1)


    @pl.when(level < EARLY)
    def _():
        pl.semaphore_wait(all_sem, 1)
        send_pages(EARLY, TOP - 1)

    arrive(AUX)
    aux_all = aux_r[...].reshape(SPAN, 128)
    rows, lanes = iota((128, 128), 0), iota((128, 128), 1)
    pick = ((rows == 6 * h + lanes) & (lanes < 6)).astype(BF16)
    own_logit = dot_nn(aux_all, pick)
    real = dot_nn(aux_all, (rows == MASK_LANE).astype(BF16))
    lane_row = iota((1, 128), 1)
    bias_row = jnp.zeros((1, 128), F32)
    rate_row = jnp.zeros((1, 128), F32)
    for j in range(6):
        bias_row = jnp.where(lane_row == j, step_bias[j], bias_row)
        rate_row = jnp.where(lane_row == j, decay_log[j], rate_row)
    rate_row = jnp.where(lane_row < 6, -jnp.exp(rate_row), 0.0)
    v = own_logit + bias_row
    steps = (jnp.maximum(v, 0.0) + jnp.log(1.0 + jnp.exp(-jnp.abs(v)))) * real
    log_decay = steps * rate_row
    causal = iota((SPAN, SPAN), 0) >= iota((SPAN, SPAN), 1)
    cumulative = jnp.dot(
        causal.astype(F32), log_decay, precision=lax.Precision.HIGHEST, preferred_element_type=F32
    )
    cumulative_t = cumulative.T
    steps_t = steps.T
    carry_weight = jnp.exp(cumulative)

    locals_[0].wait()
    locals_[5].wait()
    arrive(MAPS)
    in_map = maps_r[:, :, 0:STATE].reshape(SPAN, STATE)
    out_map = maps_r[:, :, STATE : 2 * STATE].reshape(SPAN, STATE)
    inter = dot_nt(out_map, in_map)
    locals_[1].wait()
    arrive(XS)
    for j in range(6):
        cols = pl.ds(j * HD, HD)
        gap = cumulative[:, j : j + 1] - cumulative_t[j : j + 1, :]
        weights = jnp.where(causal, jnp.exp(gap), 0.0) * inter * steps_t[j : j + 1, :]
        x = xs_r[:, :, cols].reshape(SPAN, HD)
        from_state = dot_nt(out_map, prior_v[pl.ds(j * HD, HD), :])
        result = dot_nn(weights.astype(BF16), x) + from_state * carry_weight[:, j : j + 1]
        result = (result + skip_gain[j] * x.astype(F32)) * real
        scan_s[:, :, cols] = result.astype(BF16).reshape(NX, TOK, HD)

    for k in order:
        sends[SCAN, k] = remote(SCAN, k, scan_s.at[(h + k) % NX], scan_r.at[h])
        sends[SCAN, k].start()


    one_hot = (page_map[...] == rows).astype(BF16)
    page_of = dot_nt(iota((8, 128), 1).astype(BF16), one_hot)
    expand = (iota((128, CACHED), 1) // 8 == iota((128, CACHED), 0)).astype(BF16)
    position = dot_nn(page_of.astype(BF16), expand)[0:1, :] * 16.0
    position = position + (half * 8 + iota((1, CACHED), 1) % 8).astype(F32)
    cache_bias = jnp.where(position < length[...].astype(F32), 0.0, NEG)
    slot_row = dot_nt((iota((8, 128), 1) == MASK_LANE).astype(BF16), aux_all)

    def slot_of(key):
        return (key // 32) * TOK + half * 32 + key % 32

    pick_slot = (iota((SPAN, FRESH), 0) == slot_of(iota((SPAN, FRESH), 1))).astype(BF16)
    real_row = dot_nn(slot_row.astype(BF16), pick_slot)[0:1, :]
    seen = (slot_of(iota((SPAN, FRESH), 1)) <= iota((SPAN, FRESH), 0)) & (real_row > 0.5)
    fresh_bias = jnp.where(seen, 0.0, NEG)

    near = FRESH + 8 * SPLIT
    first, last = pl.ds(0, near), pl.ds(near, CACHED + FRESH - near)
    first_bias = jnp.concatenate(
        [fresh_bias, jnp.broadcast_to(cache_bias[:, 0 : 8 * SPLIT], (SPAN, 8 * SPLIT))], axis=1
    )
    last_bias = cache_bias[:, 8 * SPLIT : CACHED]
    locals_[2].wait()
    locals_[3].wait()
    arrive(KV)
    keys[pl.ds(0, FRESH), :] = kv_r[:, :, 0:HD].reshape(FRESH, HD)
    values[pl.ds(0, FRESH), :] = kv_r[:, :, HD : 2 * HD].reshape(FRESH, HD)
    arrive(Q)
    settle(0)
    keys[pl.ds(FRESH, 8 * SPLIT), :] = pages[0:SPLIT, :, 0:HD].reshape(8 * SPLIT, HD)
    values[pl.ds(FRESH, 8 * SPLIT), :] = pages[0:SPLIT, :, HD : 2 * HD].reshape(8 * SPLIT, HD)
    tops, totals = [], []
    for j in range(6):
        query = q_r[:, :, pl.ds(j * HD, HD)].reshape(SPAN, HD)
        scores = dot_nt(query, keys[first, :]) + first_bias
        top = jnp.max(scores, axis=1, keepdims=True)
        terms = jnp.exp2((scores - top) * SCALE)
        tops.append(top)
        totals.append(jnp.sum(terms, axis=1, keepdims=True))
        partial[j] = dot_nn(terms.astype(BF16), values[first, :])

    settle(1)
    keys[last, :] = pages[SPLIT:NDP, :, 0:HD].reshape(CACHED - 8 * SPLIT, HD)
    values[last, :] = pages[SPLIT:NDP, :, HD : 2 * HD].reshape(CACHED - 8 * SPLIT, HD)
    per = 6 // PARTS
    for part in range(PARTS):
        lse = jnp.zeros((SPAN, 128), F32)
        for j in range(part * per, (part + 1) * per):
            cols = pl.ds(j * HD, HD)
            query = q_r[:, :, cols].reshape(SPAN, HD)
            scores = dot_nt(query, keys[last, :]) + last_bias
            top = jnp.maximum(tops[j], jnp.max(scores, axis=1, keepdims=True))
            terms = jnp.exp2((scores - top) * SCALE)
            before = jnp.exp2((tops[j] - top) * SCALE)
            total = totals[j] * before + jnp.sum(terms, axis=1, keepdims=True)
            weighted = partial[j] * before + dot_nn(terms.astype(BF16), values[last, :])
            att_s[part, :, :, pl.ds((j - part * per) * HD, HD)] = (weighted / total).astype(BF16).reshape(NX, TOK, HD)
            lse = jnp.where(
                iota((SPAN, 128), 1) == j - part * per, top * SCALE + jnp.log2(total), lse
            )
        for u in range(NX):
            lse_s[part, u] = lse[u * TOK : (u + 1) * TOK, :].T[0:8, :]
        for k in order:
            to = (h + k) % NX
            sends[LSE + part, k] = remote(LSE + part, k, lse_s.at[part, to], lse_r.at[part, h])
            sends[LSE + part, k].start()
            sends[ATT + part, k] = remote(
                ATT + part, k, att_s.at[part, to], att_r.at[part, h]
            )
            sends[ATT + part, k].start()

    locals_[6].wait()
    scan_r[h] = scan_s[h]
    arrive(SCAN)
    squares = jnp.zeros((TOK, 1), F32)
    for u in range(NX):
        z_in = gate_v[:, pl.ds(u * GW, GW)].astype(F32)
        gated = scan_r[u].astype(F32) * (z_in / (1.0 + jnp.exp(-z_in)))
        squares = squares + jnp.sum(gated * gated, axis=1, keepdims=True)
    inverse = lax.rsqrt(squares / MI + EPSILON)
    for u in range(NX):
        z_in = gate_v[:, pl.ds(u * GW, GW)].astype(F32)
        gated = scan_r[u].astype(F32) * (z_in / (1.0 + jnp.exp(-z_in)))
        normed = gated * inverse * norm_gain[:, pl.ds(u * GW, GW)]
        out[:, pl.ds(QH * HD + u * GW, GW)] = normed.astype(BF16)

    for part in range(PARTS):
        att_r[part, h] = att_s[part, h]
        lse_r[part, h] = lse_s[part, h]
        arrive(LSE + part)
        arrive(ATT + part)
        lse_all = lse_r[part].reshape(32, TOK).T
        for group in range(2):
            a, b = 2 * group, 2 * group + 1
            for i in range(per):
                one = lse_all[:, a * 8 + i : a * 8 + i + 1]
                two = lse_all[:, b * 8 + i : b * 8 + i + 1]
                cols = pl.ds(i * HD, HD)
                joined = att_r[part, a, :, cols].astype(F32) * (own_mask / (1.0 + jnp.exp2(two - one)))
                joined = joined + att_r[part, b, :, cols].astype(F32) * (
                    own_mask / (1.0 + jnp.exp2(one - two))
                )
                out[:, pl.ds(group * GW + (part * per + i) * HD, HD)] = joined.astype(BF16)

    for copy in sends.values():
        copy.wait_send()
    pltpu.make_async_remote_copy(
        src_ref=pool.at[pl.ds(0, NDP - 1)],
        dst_ref=pages.at[pl.ds(0, NDP - 1)],
        send_sem=page_send,
        recv_sem=page_recv.at[0],
        device_id=(d, (h + 1) % NX),
        device_id_type=MESH,
    ).wait_send()


def local(
    queries, fresh_keyvals, ssm_input, gate_input, state_maps, step_logit, slot_mask, cache_pool,
    page_map, cached_lengths, prior_state, decay_log, step_bias, skip_gain, norm_gain,
):
    hbm = pl.BlockSpec(memory_space=pl.ANY)
    vmem = pl.BlockSpec(memory_space=pltpu.VMEM)
    smem = pl.BlockSpec(memory_space=pltpu.SMEM)
    return pl.pallas_call(
        kernel,
        out_shape=pltpu.VMEM((TOK, QH * HD + MI), BF16),
        in_specs=[
            hbm, hbm, hbm, hbm, hbm, vmem, vmem, hbm, vmem, vmem, hbm, smem, smem, smem, vmem,
        ],
        out_specs=vmem,
        scratch_shapes=[
            pltpu.VMEM((TOK, 128), BF16),
            pltpu.VMEM((NX, TOK, 128), BF16),
            pltpu.VMEM((NX, TOK, 2 * STATE), BF16),
            pltpu.VMEM((NX, TOK, GW), BF16),
            pltpu.VMEM((NX, 32, 2 * HD), BF16),
            pltpu.VMEM((NX, TOK, GW), BF16),
            pltpu.VMEM((NDP, 8, 2 * HD), BF16),
            pltpu.VMEM((GW, STATE), BF16),
            pltpu.VMEM((TOK, MI), BF16),
            pltpu.VMEM((NX, TOK, GW), BF16),
            pltpu.VMEM((NX, TOK, GW), BF16),
            pltpu.VMEM((PARTS, NX, TOK, GW // PARTS), BF16),
            pltpu.VMEM((PARTS, NX, TOK, GW // PARTS), BF16),
            pltpu.VMEM((PARTS, NX, 8, TOK), F32),
            pltpu.VMEM((PARTS, NX, 8, TOK), F32),
            pltpu.VMEM((6, SPAN, HD), F32),
            pltpu.VMEM((CACHED + FRESH, HD), BF16),
            pltpu.VMEM((CACHED + FRESH, HD), BF16),
            pltpu.SemaphoreType.DMA((KINDS, NX)),
            pltpu.SemaphoreType.DMA((KINDS, NX)),
            pltpu.SemaphoreType.DMA,
            pltpu.SemaphoreType.DMA((2,)),
            pltpu.SemaphoreType.DMA((6,)),
            pltpu.SemaphoreType.REGULAR,
            pltpu.SemaphoreType.REGULAR,
        ],
        compiler_params=pltpu.CompilerParams(collective_id=0, has_side_effects=True),
        name="mixer",
    )(
        queries, fresh_keyvals, ssm_input, gate_input, state_maps, step_logit.T,
        slot_mask.reshape(1, TOK), cache_pool, page_map, cached_lengths.reshape(1, 1),
        prior_state.reshape(GW, STATE), decay_log, step_bias, skip_gain, norm_gain.reshape(1, MI),
    )


def solution(mesh):
    tokens = P(("dp", "head"), None)
    in_specs = (
        tokens, tokens, tokens, tokens, tokens, tokens,
        P(("dp", "head")),
        P("dp", "head", None),
        P("dp", None),
        P("dp"),
        P("dp", "head", None, None),
        P("head"), P("head"), P("head"),
        P(),
    )
    return jax.shard_map(
        local, mesh=mesh, in_specs=in_specs, out_specs=tokens, check_vma=False
    )
```

```python
import math

import jax
import jax.numpy as jnp
from jax import lax
from jax.experimental import pallas as pl
from jax.experimental.pallas import tpu as pltpu
from jax.sharding import PartitionSpec as P

HD = 128
QH = 12
STATE = 256
MI = 3072
EPSILON = 1e-05
NX = 4
NDP = 128
NY = 8
NZ = 8
TOK = 64
SPAN = 256
GW = 768
CACHED = 1024
FRESH = 128
MASK_LANE = 24
NEG = -1e30
LOG2E = 1.4426950408889634
SCALE = LOG2E / math.sqrt(HD)
MESH = pl.DeviceIdType.MESH
F32 = jnp.float32
BF16 = jnp.bfloat16
PARTS = 3
AUX, MAPS, XS, KV, Q, SCAN, ATT, LSE = 0, 1, 2, 3, 4, 5, 6, 6 + PARTS
KINDS = LSE + PARTS


def iota(shape, axis):
    return lax.broadcasted_iota(jnp.int32, shape, axis)


def level_of(device):
    z, y = device >> 4, (device >> 1) & 7
    return z + (y >> 2) + (z >> 2) * (1 + 3 * (y >> 2)) + 2 * (device < 1)


LEVELS = [level_of(t) for t in range(NDP)]
TOP = 13
MEMBERS = [LEVELS.count(value) for value in range(TOP)]
EARLY = 5
SPLIT = sum(MEMBERS[:EARLY])


def dot_nt(a, b):
    return lax.dot_general(a, b, (((1,), (1,)), ((), ())), preferred_element_type=F32)


def dot_nn(a, b):
    return jnp.dot(a, b, preferred_element_type=F32)


def kernel(
    q, kv, xs, gate, maps, logit, mask, pool, page_map, length, prior, decay_log, step_bias,
    skip_gain, norm_gain, out,
    aux_own, aux_r, maps_r, xs_r, kv_r, q_r, pages, prior_v, gate_v, scan_s, scan_r, att_s, att_r,
    lse_s, lse_r, partial, keys, values, send_sem, recv_sem, page_send, page_recv, local_sem, early_sem,
    all_sem,
):
    d = lax.axis_index("dp")
    h = lax.axis_index("head")
    g, half = h // 2, h % 2
    level = level_of(d)
    side = (level >= EARLY).astype(jnp.int32)
    barrier = pltpu.get_barrier_semaphore()

    for k in range(1, NX):
        pl.semaphore_signal(barrier, 1, device_id=(d, (h + k) % NX), device_id_type=MESH)
    for t in sorted(range(NDP), key=lambda t: LEVELS[t]):

        @pl.when((level <= LEVELS[t]) & (d != t))
        def _():
            pl.semaphore_signal(barrier, 1, device_id=(t, h), device_id_type=MESH)

    greeted = NX - 1 - 1
    for value in range(TOP):
        greeted = greeted + jnp.where(level >= value, MEMBERS[value], 0)

    def group_cols(ref, index):
        return ref.at[:, pl.ds(pl.multiple_of(index * GW, 128), GW)]

    def fresh_part(index):
        return kv.at[
            pl.ds(pl.multiple_of((index % 2) * 32, 32), 32),
            pl.ds(pl.multiple_of((index // 2) * 256, 128), 256),
        ]

    locals_ = [
        pltpu.make_async_copy(maps, maps_r.at[h], local_sem.at[0]),
        pltpu.make_async_copy(group_cols(xs, h), xs_r.at[h], local_sem.at[1]),
        pltpu.make_async_copy(fresh_part(h), kv_r.at[h], local_sem.at[2]),
        pltpu.make_async_copy(group_cols(q, g), q_r.at[h], local_sem.at[3]),
        pltpu.make_async_copy(pool.at[d], pages.at[d], page_recv.at[side]),
        pltpu.make_async_copy(prior, prior_v, local_sem.at[4]),
        pltpu.make_async_copy(gate, gate_v, local_sem.at[5]),
    ]
    for copy in locals_:
        copy.start()

    eye = iota((TOK, TOK), 0) == iota((TOK, TOK), 1)
    own_mask = jnp.where(eye, jnp.broadcast_to(mask[...].astype(F32), (TOK, TOK)), 0.0)
    own_mask = jnp.sum((own_mask > 0.5).astype(F32), axis=1, keepdims=True)
    spread = (iota((24, 128), 0) == iota((24, 128), 1)).astype(BF16)
    aux = lax.dot_general(
        logit[...], spread, (((0,), (0,)), ((), ())), preferred_element_type=F32
    )
    aux = jnp.where(iota((TOK, 128), 1) == MASK_LANE, own_mask, aux).astype(BF16)
    aux_own[...] = aux
    aux_r[h] = aux

    pl.semaphore_wait(barrier, greeted)

    @pl.when(level == EARLY - 1)
    def _():
        for k in range(7):
            target = d - 56 + 8 * k
            pl.semaphore_signal(early_sem, 1, device_id=(target, h), device_id_type=MESH)

    @pl.when(level == TOP - 1)
    def _():
        for k in range(15):
            target = d - 120 + 8 * k
            pl.semaphore_signal(all_sem, 1, device_id=(target, h), device_id_type=MESH)

    def remote(kind, k, src, dst):
        return pltpu.make_async_remote_copy(
            src_ref=src,
            dst_ref=dst,
            send_sem=send_sem.at[kind, k],
            recv_sem=recv_sem.at[kind, k],
            device_id=(d, (h + k) % NX),
            device_id_type=MESH,
        )

    order = (2, 1, 3)
    sends = {}
    for k in order:
        sends[AUX, k] = remote(AUX, k, aux_own, aux_r.at[h])
    for k in order:
        sends[MAPS, k] = remote(MAPS, k, maps, maps_r.at[h])
    for k in order:
        sends[XS, k] = remote(XS, k, group_cols(xs, (h + k) % NX), xs_r.at[h])
    for k in order:
        sends[KV, k] = remote(KV, k, fresh_part((h + k) % NX), kv_r.at[h])
    for k in order:
        sends[Q, k] = remote(Q, k, group_cols(q, ((h + k) % NX) // 2), q_r.at[h])

    def send_pages(low, high):
        def step(i, carry):
            target = (d + i * 45) & (NDP - 1)
            other = level_of(target)

            @pl.when((other >= low) & (other <= high))
            def _():
                pltpu.make_async_remote_copy(
                    src_ref=pool.at[target],
                    dst_ref=pages.at[d],
                    send_sem=page_send,
                    recv_sem=page_recv.at[side],
                    device_id=(target, h),
                    device_id_type=MESH,
                ).start()

            return carry

        lax.fori_loop(1, NDP, step, 0)

    def settle(j):
        part = pl.ds(0, SPLIT if j == 0 else NDP - SPLIT)
        pltpu.make_async_copy(pool.at[part], pages.at[part], page_recv.at[j]).wait()

    send_pages(0, jnp.minimum(level, 1))

    @pl.when(level >= 2)
    def _():
        send_pages(2, jnp.minimum(level, EARLY - 1))


    for copy in sends.values():
        copy.start()

    @pl.when(level >= EARLY)
    def _():
        send_pages(EARLY, level)


    def arrive(kind):
        for k in order:
            sends[kind, k].wait_recv()

    @pl.when(level < EARLY - 1)
    def _():
        pl.semaphore_wait(early_sem, 1)
        send_pages(level + 1, EARLY - 1)


    @pl.when(level < EARLY)
    def _():
        pl.semaphore_wait(all_sem, 1)
        send_pages(EARLY, TOP - 1)

    arrive(AUX)
    aux_all = aux_r[...].reshape(SPAN, 128)
    rows, lanes = iota((128, 128), 0), iota((128, 128), 1)
    pick = ((rows == 6 * h + lanes) & (lanes < 6)).astype(BF16)
    own_logit = dot_nn(aux_all, pick)
    real = dot_nn(aux_all, (rows == MASK_LANE).astype(BF16))
    lane_row = iota((1, 128), 1)
    bias_row = jnp.zeros((1, 128), F32)
    rate_row = jnp.zeros((1, 128), F32)
    for j in range(6):
        bias_row = jnp.where(lane_row == j, step_bias[j], bias_row)
        rate_row = jnp.where(lane_row == j, decay_log[j], rate_row)
    rate_row = jnp.where(lane_row < 6, -jnp.exp(rate_row), 0.0)
    v = own_logit + bias_row
    steps = (jnp.maximum(v, 0.0) + jnp.log(1.0 + jnp.exp(-jnp.abs(v)))) * real
    log_decay = steps * rate_row
    causal = iota((SPAN, SPAN), 0) >= iota((SPAN, SPAN), 1)
    cumulative = jnp.dot(
        causal.astype(F32), log_decay, precision=lax.Precision.HIGHEST, preferred_element_type=F32
    )
    cumulative_t = cumulative.T
    steps_t = steps.T
    carry_weight = jnp.exp(cumulative)

    locals_[0].wait()
    locals_[5].wait()
    arrive(MAPS)
    in_map = maps_r[:, :, 0:STATE].reshape(SPAN, STATE)
    out_map = maps_r[:, :, STATE : 2 * STATE].reshape(SPAN, STATE)
    inter = dot_nt(out_map, in_map)
    locals_[1].wait()
    arrive(XS)
    for j in range(6):
        cols = pl.ds(j * HD, HD)
        gap = cumulative[:, j : j + 1] - cumulative_t[j : j + 1, :]
        weights = jnp.where(causal, jnp.exp(gap), 0.0) * inter * steps_t[j : j + 1, :]
        x = xs_r[:, :, cols].reshape(SPAN, HD)
        from_state = dot_nt(out_map, prior_v[pl.ds(j * HD, HD), :])
        result = dot_nn(weights.astype(BF16), x) + from_state * carry_weight[:, j : j + 1]
        result = (result + skip_gain[j] * x.astype(F32)) * real
        scan_s[:, :, cols] = result.astype(BF16).reshape(NX, TOK, HD)

    for k in order:
        sends[SCAN, k] = remote(SCAN, k, scan_s.at[(h + k) % NX], scan_r.at[h])
        sends[SCAN, k].start()


    @pl.when((level >= EARLY) & (level < TOP - 1))
    def _():
        pl.semaphore_wait(all_sem, 1)
        send_pages(level + 1, TOP - 1)

    one_hot = (page_map[...] == rows).astype(BF16)
    page_of = dot_nt(iota((8, 128), 1).astype(BF16), one_hot)
    expand = (iota((128, CACHED), 1) // 8 == iota((128, CACHED), 0)).astype(BF16)
    position = dot_nn(page_of.astype(BF16), expand)[0:1, :] * 16.0
    position = position + (half * 8 + iota((1, CACHED), 1) % 8).astype(F32)
    cache_bias = jnp.where(position < length[...].astype(F32), 0.0, NEG)
    slot_row = dot_nt((iota((8, 128), 1) == MASK_LANE).astype(BF16), aux_all)

    def slot_of(key):
        return (key // 32) * TOK + half * 32 + key % 32

    pick_slot = (iota((SPAN, FRESH), 0) == slot_of(iota((SPAN, FRESH), 1))).astype(BF16)
    real_row = dot_nn(slot_row.astype(BF16), pick_slot)[0:1, :]
    seen = (slot_of(iota((SPAN, FRESH), 1)) <= iota((SPAN, FRESH), 0)) & (real_row > 0.5)
    fresh_bias = jnp.where(seen, 0.0, NEG)

    near = FRESH + 8 * SPLIT
    first, last = pl.ds(0, near), pl.ds(near, CACHED + FRESH - near)
    first_bias = jnp.concatenate(
        [fresh_bias, jnp.broadcast_to(cache_bias[:, 0 : 8 * SPLIT], (SPAN, 8 * SPLIT))], axis=1
    )
    last_bias = cache_bias[:, 8 * SPLIT : CACHED]
    locals_[2].wait()
    locals_[3].wait()
    arrive(KV)
    keys[pl.ds(0, FRESH), :] = kv_r[:, :, 0:HD].reshape(FRESH, HD)
    values[pl.ds(0, FRESH), :] = kv_r[:, :, HD : 2 * HD].reshape(FRESH, HD)
    arrive(Q)
    settle(0)
    keys[pl.ds(FRESH, 8 * SPLIT), :] = pages[0:SPLIT, :, 0:HD].reshape(8 * SPLIT, HD)
    values[pl.ds(FRESH, 8 * SPLIT), :] = pages[0:SPLIT, :, HD : 2 * HD].reshape(8 * SPLIT, HD)
    tops, totals = [], []
    for j in range(6):
        query = q_r[:, :, pl.ds(j * HD, HD)].reshape(SPAN, HD)
        scores = dot_nt(query, keys[first, :]) + first_bias
        top = jnp.max(scores, axis=1, keepdims=True)
        terms = jnp.exp2((scores - top) * SCALE)
        tops.append(top)
        totals.append(jnp.sum(terms, axis=1, keepdims=True))
        partial[j] = dot_nn(terms.astype(BF16), values[first, :])

    settle(1)
    keys[last, :] = pages[SPLIT:NDP, :, 0:HD].reshape(CACHED - 8 * SPLIT, HD)
    values[last, :] = pages[SPLIT:NDP, :, HD : 2 * HD].reshape(CACHED - 8 * SPLIT, HD)
    per = 6 // PARTS
    for part in range(PARTS):
        lse = jnp.zeros((SPAN, 128), F32)
        for j in range(part * per, (part + 1) * per):
            cols = pl.ds(j * HD, HD)
            query = q_r[:, :, cols].reshape(SPAN, HD)
            scores = dot_nt(query, keys[last, :]) + last_bias
            top = jnp.maximum(tops[j], jnp.max(scores, axis=1, keepdims=True))
            terms = jnp.exp2((scores - top) * SCALE)
            before = jnp.exp2((tops[j] - top) * SCALE)
            total = totals[j] * before + jnp.sum(terms, axis=1, keepdims=True)
            weighted = partial[j] * before + dot_nn(terms.astype(BF16), values[last, :])
            att_s[part, :, :, pl.ds((j - part * per) * HD, HD)] = (weighted / total).astype(BF16).reshape(NX, TOK, HD)
            lse = jnp.where(
                iota((SPAN, 128), 1) == j - part * per, top * SCALE + jnp.log2(total), lse
            )
        for u in range(NX):
            lse_s[part, u] = lse[u * TOK : (u + 1) * TOK, :].T[0:8, :]
        for k in order:
            to = (h + k) % NX
            sends[LSE + part, k] = remote(LSE + part, k, lse_s.at[part, to], lse_r.at[part, h])
            sends[LSE + part, k].start()
            sends[ATT + part, k] = remote(
                ATT + part, k, att_s.at[part, to], att_r.at[part, h]
            )
            sends[ATT + part, k].start()

    locals_[6].wait()
    scan_r[h] = scan_s[h]
    arrive(SCAN)
    squares = jnp.zeros((TOK, 1), F32)
    for u in range(NX):
        z_in = gate_v[:, pl.ds(u * GW, GW)].astype(F32)
        gated = scan_r[u].astype(F32) * (z_in / (1.0 + jnp.exp(-z_in)))
        squares = squares + jnp.sum(gated * gated, axis=1, keepdims=True)
    inverse = lax.rsqrt(squares / MI + EPSILON)
    for u in range(NX):
        z_in = gate_v[:, pl.ds(u * GW, GW)].astype(F32)
        gated = scan_r[u].astype(F32) * (z_in / (1.0 + jnp.exp(-z_in)))
        normed = gated * inverse * norm_gain[:, pl.ds(u * GW, GW)]
        out[:, pl.ds(QH * HD + u * GW, GW)] = normed.astype(BF16)

    for part in range(PARTS):
        att_r[part, h] = att_s[part, h]
        lse_r[part, h] = lse_s[part, h]
        arrive(LSE + part)
        arrive(ATT + part)
        lse_all = lse_r[part].reshape(32, TOK).T
        for group in range(2):
            a, b = 2 * group, 2 * group + 1
            for i in range(per):
                one = lse_all[:, a * 8 + i : a * 8 + i + 1]
                two = lse_all[:, b * 8 + i : b * 8 + i + 1]
                cols = pl.ds(i * HD, HD)
                joined = att_r[part, a, :, cols].astype(F32) * (own_mask / (1.0 + jnp.exp2(two - one)))
                joined = joined + att_r[part, b, :, cols].astype(F32) * (
                    own_mask / (1.0 + jnp.exp2(one - two))
                )
                out[:, pl.ds(group * GW + (part * per + i) * HD, HD)] = joined.astype(BF16)

    for copy in sends.values():
        copy.wait_send()
    pltpu.make_async_remote_copy(
        src_ref=pool.at[pl.ds(0, NDP - 1)],
        dst_ref=pages.at[pl.ds(0, NDP - 1)],
        send_sem=page_send,
        recv_sem=page_recv.at[0],
        device_id=(d, (h + 1) % NX),
        device_id_type=MESH,
    ).wait_send()


def local(
    queries, fresh_keyvals, ssm_input, gate_input, state_maps, step_logit, slot_mask, cache_pool,
    page_map, cached_lengths, prior_state, decay_log, step_bias, skip_gain, norm_gain,
):
    hbm = pl.BlockSpec(memory_space=pl.ANY)
    vmem = pl.BlockSpec(memory_space=pltpu.VMEM)
    smem = pl.BlockSpec(memory_space=pltpu.SMEM)
    return pl.pallas_call(
        kernel,
        out_shape=pltpu.VMEM((TOK, QH * HD + MI), BF16),
        in_specs=[
            hbm, hbm, hbm, hbm, hbm, vmem, vmem, hbm, vmem, vmem, hbm, smem, smem, smem, vmem,
        ],
        out_specs=vmem,
        scratch_shapes=[
            pltpu.VMEM((TOK, 128), BF16),
            pltpu.VMEM((NX, TOK, 128), BF16),
            pltpu.VMEM((NX, TOK, 2 * STATE), BF16),
            pltpu.VMEM((NX, TOK, GW), BF16),
            pltpu.VMEM((NX, 32, 2 * HD), BF16),
            pltpu.VMEM((NX, TOK, GW), BF16),
            pltpu.VMEM((NDP, 8, 2 * HD), BF16),
            pltpu.VMEM((GW, STATE), BF16),
            pltpu.VMEM((TOK, MI), BF16),
            pltpu.VMEM((NX, TOK, GW), BF16),
            pltpu.VMEM((NX, TOK, GW), BF16),
            pltpu.VMEM((PARTS, NX, TOK, GW // PARTS), BF16),
            pltpu.VMEM((PARTS, NX, TOK, GW // PARTS), BF16),
            pltpu.VMEM((PARTS, NX, 8, TOK), F32),
            pltpu.VMEM((PARTS, NX, 8, TOK), F32),
            pltpu.VMEM((6, SPAN, HD), F32),
            pltpu.VMEM((CACHED + FRESH, HD), BF16),
            pltpu.VMEM((CACHED + FRESH, HD), BF16),
            pltpu.SemaphoreType.DMA((KINDS, NX)),
            pltpu.SemaphoreType.DMA((KINDS, NX)),
            pltpu.SemaphoreType.DMA,
            pltpu.SemaphoreType.DMA((2,)),
            pltpu.SemaphoreType.DMA((6,)),
            pltpu.SemaphoreType.REGULAR,
            pltpu.SemaphoreType.REGULAR,
        ],
        compiler_params=pltpu.CompilerParams(collective_id=0, has_side_effects=True),
        name="mixer",
    )(
        queries, fresh_keyvals, ssm_input, gate_input, state_maps, step_logit.T,
        slot_mask.reshape(1, TOK), cache_pool, page_map, cached_lengths.reshape(1, 1),
        prior_state.reshape(GW, STATE), decay_log, step_bias, skip_gain, norm_gain.reshape(1, MI),
    )


def solution(mesh):
    tokens = P(("dp", "head"), None)
    in_specs = (
        tokens, tokens, tokens, tokens, tokens, tokens,
        P(("dp", "head")),
        P("dp", "head", None),
        P("dp", None),
        P("dp"),
        P("dp", "head", None, None),
        P("head"), P("head"), P("head"),
        P(),
    )
    return jax.shard_map(
        local, mesh=mesh, in_specs=in_specs, out_specs=tokens, check_vma=False
    )
```

```python
import math

import jax
import jax.numpy as jnp
from jax import lax
from jax.experimental import pallas as pl
from jax.experimental.pallas import tpu as pltpu
from jax.sharding import PartitionSpec as P

HD = 128
QH = 12
STATE = 256
MI = 3072
EPSILON = 1e-05
NX = 4
NDP = 128
NY = 8
NZ = 8
TOK = 64
SPAN = 256
GW = 768
CACHED = 1024
FRESH = 128
MASK_LANE = 24
NEG = -1e30
LOG2E = 1.4426950408889634
SCALE = LOG2E / math.sqrt(HD)
MESH = pl.DeviceIdType.MESH
F32 = jnp.float32
BF16 = jnp.bfloat16
PARTS = 3
AUX, MAPS, XS, KV, Q, SCAN, ATT, LSE = 0, 1, 2, 3, 4, 5, 6, 6 + PARTS
KINDS = LSE + PARTS


def iota(shape, axis):
    return lax.broadcasted_iota(jnp.int32, shape, axis)


def level_of(device):
    z, y = device >> 4, (device >> 1) & 7
    return z + (y >> 2) + (z >> 2) * (1 + 3 * (y >> 2)) + 2 * (device < 1)


LEVELS = [level_of(t) for t in range(NDP)]
TOP = 13
MEMBERS = [LEVELS.count(value) for value in range(TOP)]
EARLY = 5
SPLIT = sum(MEMBERS[:EARLY])


def dot_nt(a, b):
    return lax.dot_general(a, b, (((1,), (1,)), ((), ())), preferred_element_type=F32)


def dot_nn(a, b):
    return jnp.dot(a, b, preferred_element_type=F32)


def kernel(
    q, kv, xs, gate, maps, logit, mask, pool, page_map, length, prior, decay_log, step_bias,
    skip_gain, norm_gain, out,
    aux_own, aux_r, maps_r, xs_r, kv_r, q_r, pages, prior_v, gate_v, scan_s, scan_r, att_s, att_r,
    lse_s, lse_r, partial, keys, values, send_sem, recv_sem, page_send, page_recv, local_sem, early_sem,
    all_sem,
):
    d = lax.axis_index("dp")
    h = lax.axis_index("head")
    g, half = h // 2, h % 2
    level = level_of(d)
    side = (level >= EARLY).astype(jnp.int32)
    barrier = pltpu.get_barrier_semaphore()

    for k in range(1, NX):
        pl.semaphore_signal(barrier, 1, device_id=(d, (h + k) % NX), device_id_type=MESH)
    for t in sorted(range(NDP), key=lambda t: LEVELS[t]):

        @pl.when((level <= LEVELS[t]) & (d != t))
        def _():
            pl.semaphore_signal(barrier, 1, device_id=(t, h), device_id_type=MESH)

    greeted = NX - 1 - 1
    for value in range(TOP):
        greeted = greeted + jnp.where(level >= value, MEMBERS[value], 0)

    def group_cols(ref, index):
        return ref.at[:, pl.ds(pl.multiple_of(index * GW, 128), GW)]

    def fresh_part(index):
        return kv.at[
            pl.ds(pl.multiple_of((index % 2) * 32, 32), 32),
            pl.ds(pl.multiple_of((index // 2) * 256, 128), 256),
        ]

    locals_ = [
        pltpu.make_async_copy(maps, maps_r.at[h], local_sem.at[0]),
        pltpu.make_async_copy(group_cols(xs, h), xs_r.at[h], local_sem.at[1]),
        pltpu.make_async_copy(fresh_part(h), kv_r.at[h], local_sem.at[2]),
        pltpu.make_async_copy(group_cols(q, g), q_r.at[h], local_sem.at[3]),
        pltpu.make_async_copy(pool.at[d], pages.at[d], page_recv.at[side]),
        pltpu.make_async_copy(prior, prior_v, local_sem.at[4]),
        pltpu.make_async_copy(gate, gate_v, local_sem.at[5]),
    ]
    for copy in locals_:
        copy.start()

    eye = iota((TOK, TOK), 0) == iota((TOK, TOK), 1)
    own_mask = jnp.where(eye, jnp.broadcast_to(mask[...].astype(F32), (TOK, TOK)), 0.0)
    own_mask = jnp.sum((own_mask > 0.5).astype(F32), axis=1, keepdims=True)
    spread = (iota((24, 128), 0) == iota((24, 128), 1)).astype(BF16)
    aux = lax.dot_general(
        logit[...], spread, (((0,), (0,)), ((), ())), preferred_element_type=F32
    )
    aux = jnp.where(iota((TOK, 128), 1) == MASK_LANE, own_mask, aux).astype(BF16)
    aux_own[...] = aux
    aux_r[h] = aux

    pl.semaphore_wait(barrier, greeted)

    @pl.when(level == EARLY - 1)
    def _():
        for k in range(7):
            target = d - 56 + 8 * k
            pl.semaphore_signal(early_sem, 1, device_id=(target, h), device_id_type=MESH)

    @pl.when(level == TOP - 1)
    def _():
        for k in range(15):
            target = d - 120 + 8 * k
            pl.semaphore_signal(all_sem, 1, device_id=(target, h), device_id_type=MESH)

    def remote(kind, k, src, dst):
        return pltpu.make_async_remote_copy(
            src_ref=src,
            dst_ref=dst,
            send_sem=send_sem.at[kind, k],
            recv_sem=recv_sem.at[kind, k],
            device_id=(d, (h + k) % NX),
            device_id_type=MESH,
        )

    order = (2, 1, 3)
    sends = {}
    for k in order:
        sends[AUX, k] = remote(AUX, k, aux_own, aux_r.at[h])
    for k in order:
        sends[MAPS, k] = remote(MAPS, k, maps, maps_r.at[h])
    for k in order:
        sends[XS, k] = remote(XS, k, group_cols(xs, (h + k) % NX), xs_r.at[h])
    for k in order:
        sends[KV, k] = remote(KV, k, fresh_part((h + k) % NX), kv_r.at[h])
    for k in order:
        sends[Q, k] = remote(Q, k, group_cols(q, ((h + k) % NX) // 2), q_r.at[h])

    def send_pages(low, high):
        def step(i, carry):
            target = (d + i * 75) & (NDP - 1)
            other = level_of(target)

            @pl.when((other >= low) & (other <= high))
            def _():
                pltpu.make_async_remote_copy(
                    src_ref=pool.at[target],
                    dst_ref=pages.at[d],
                    send_sem=page_send,
                    recv_sem=page_recv.at[side],
                    device_id=(target, h),
                    device_id_type=MESH,
                ).start()

            return carry

        lax.fori_loop(1, NDP, step, 0)

    def settle(j):
        part = pl.ds(0, SPLIT if j == 0 else NDP - SPLIT)
        pltpu.make_async_copy(pool.at[part], pages.at[part], page_recv.at[j]).wait()

    send_pages(0, jnp.minimum(level, 1))

    @pl.when(level >= 2)
    def _():
        send_pages(2, jnp.minimum(level, EARLY - 1))


    for copy in sends.values():
        copy.start()

    @pl.when(level >= EARLY)
    def _():
        send_pages(EARLY, level)


    def arrive(kind):
        for k in order:
            sends[kind, k].wait_recv()

    @pl.when(level < EARLY - 1)
    def _():
        pl.semaphore_wait(early_sem, 1)
        send_pages(level + 1, EARLY - 1)


    @pl.when(level < EARLY)
    def _():
        pl.semaphore_wait(all_sem, 1)
        send_pages(EARLY, TOP - 1)

    arrive(AUX)
    aux_all = aux_r[...].reshape(SPAN, 128)
    rows, lanes = iota((128, 128), 0), iota((128, 128), 1)
    pick = ((rows == 6 * h + lanes) & (lanes < 6)).astype(BF16)
    own_logit = dot_nn(aux_all, pick)
    real = dot_nn(aux_all, (rows == MASK_LANE).astype(BF16))
    lane_row = iota((1, 128), 1)
    bias_row = jnp.zeros((1, 128), F32)
    rate_row = jnp.zeros((1, 128), F32)
    for j in range(6):
        bias_row = jnp.where(lane_row == j, step_bias[j], bias_row)
        rate_row = jnp.where(lane_row == j, decay_log[j], rate_row)
    rate_row = jnp.where(lane_row < 6, -jnp.exp(rate_row), 0.0)
    v = own_logit + bias_row
    steps = (jnp.maximum(v, 0.0) + jnp.log(1.0 + jnp.exp(-jnp.abs(v)))) * real
    log_decay = steps * rate_row
    causal = iota((SPAN, SPAN), 0) >= iota((SPAN, SPAN), 1)
    cumulative = jnp.dot(
        causal.astype(F32), log_decay, precision=lax.Precision.HIGHEST, preferred_element_type=F32
    )
    cumulative_t = cumulative.T
    steps_t = steps.T
    carry_weight = jnp.exp(cumulative)

    locals_[0].wait()
    locals_[5].wait()
    arrive(MAPS)
    in_map = maps_r[:, :, 0:STATE].reshape(SPAN, STATE)
    out_map = maps_r[:, :, STATE : 2 * STATE].reshape(SPAN, STATE)
    inter = dot_nt(out_map, in_map)
    locals_[1].wait()
    arrive(XS)
    for j in range(6):
        cols = pl.ds(j * HD, HD)
        gap = cumulative[:, j : j + 1] - cumulative_t[j : j + 1, :]
        weights = jnp.where(causal, jnp.exp(gap), 0.0) * inter * steps_t[j : j + 1, :]
        x = xs_r[:, :, cols].reshape(SPAN, HD)
        from_state = dot_nt(out_map, prior_v[pl.ds(j * HD, HD), :])
        result = dot_nn(weights.astype(BF16), x) + from_state * carry_weight[:, j : j + 1]
        result = (result + skip_gain[j] * x.astype(F32)) * real
        scan_s[:, :, cols] = result.astype(BF16).reshape(NX, TOK, HD)

    for k in order:
        sends[SCAN, k] = remote(SCAN, k, scan_s.at[(h + k) % NX], scan_r.at[h])
        sends[SCAN, k].start()


    @pl.when((level >= EARLY) & (level < TOP - 1))
    def _():
        pl.semaphore_wait(all_sem, 1)
        send_pages(level + 1, TOP - 1)

    one_hot = (page_map[...] == rows).astype(BF16)
    page_of = dot_nt(iota((8, 128), 1).astype(BF16), one_hot)
    expand = (iota((128, CACHED), 1) // 8 == iota((128, CACHED), 0)).astype(BF16)
    position = dot_nn(page_of.astype(BF16), expand)[0:1, :] * 16.0
    position = position + (half * 8 + iota((1, CACHED), 1) % 8).astype(F32)
    cache_bias = jnp.where(position < length[...].astype(F32), 0.0, NEG)
    slot_row = dot_nt((iota((8, 128), 1) == MASK_LANE).astype(BF16), aux_all)

    def slot_of(key):
        return (key // 32) * TOK + half * 32 + key % 32

    pick_slot = (iota((SPAN, FRESH), 0) == slot_of(iota((SPAN, FRESH), 1))).astype(BF16)
    real_row = dot_nn(slot_row.astype(BF16), pick_slot)[0:1, :]
    seen = (slot_of(iota((SPAN, FRESH), 1)) <= iota((SPAN, FRESH), 0)) & (real_row > 0.5)
    fresh_bias = jnp.where(seen, 0.0, NEG)

    near = FRESH + 8 * SPLIT
    first, last = pl.ds(0, near), pl.ds(near, CACHED + FRESH - near)
    first_bias = jnp.concatenate(
        [fresh_bias, jnp.broadcast_to(cache_bias[:, 0 : 8 * SPLIT], (SPAN, 8 * SPLIT))], axis=1
    )
    last_bias = cache_bias[:, 8 * SPLIT : CACHED]
    locals_[2].wait()
    locals_[3].wait()
    arrive(KV)
    keys[pl.ds(0, FRESH), :] = kv_r[:, :, 0:HD].reshape(FRESH, HD)
    values[pl.ds(0, FRESH), :] = kv_r[:, :, HD : 2 * HD].reshape(FRESH, HD)
    arrive(Q)
    settle(0)
    keys[pl.ds(FRESH, 8 * SPLIT), :] = pages[0:SPLIT, :, 0:HD].reshape(8 * SPLIT, HD)
    values[pl.ds(FRESH, 8 * SPLIT), :] = pages[0:SPLIT, :, HD : 2 * HD].reshape(8 * SPLIT, HD)
    tops, totals = [], []
    for j in range(6):
        query = q_r[:, :, pl.ds(j * HD, HD)].reshape(SPAN, HD)
        scores = dot_nt(query, keys[first, :]) + first_bias
        top = jnp.max(scores, axis=1, keepdims=True)
        terms = jnp.exp2((scores - top) * SCALE)
        tops.append(top)
        totals.append(jnp.sum(terms, axis=1, keepdims=True))
        partial[j] = dot_nn(terms.astype(BF16), values[first, :])

    settle(1)
    keys[last, :] = pages[SPLIT:NDP, :, 0:HD].reshape(CACHED - 8 * SPLIT, HD)
    values[last, :] = pages[SPLIT:NDP, :, HD : 2 * HD].reshape(CACHED - 8 * SPLIT, HD)
    per = 6 // PARTS
    for part in range(PARTS):
        lse = jnp.zeros((SPAN, 128), F32)
        for j in range(part * per, (part + 1) * per):
            cols = pl.ds(j * HD, HD)
            query = q_r[:, :, cols].reshape(SPAN, HD)
            scores = dot_nt(query, keys[last, :]) + last_bias
            top = jnp.maximum(tops[j], jnp.max(scores, axis=1, keepdims=True))
            terms = jnp.exp2((scores - top) * SCALE)
            before = jnp.exp2((tops[j] - top) * SCALE)
            total = totals[j] * before + jnp.sum(terms, axis=1, keepdims=True)
            weighted = partial[j] * before + dot_nn(terms.astype(BF16), values[last, :])
            att_s[part, :, :, pl.ds((j - part * per) * HD, HD)] = (weighted / total).astype(BF16).reshape(NX, TOK, HD)
            lse = jnp.where(
                iota((SPAN, 128), 1) == j - part * per, top * SCALE + jnp.log2(total), lse
            )
        for u in range(NX):
            lse_s[part, u] = lse[u * TOK : (u + 1) * TOK, :].T[0:8, :]
        for k in order:
            to = (h + k) % NX
            sends[LSE + part, k] = remote(LSE + part, k, lse_s.at[part, to], lse_r.at[part, h])
            sends[LSE + part, k].start()
            sends[ATT + part, k] = remote(
                ATT + part, k, att_s.at[part, to], att_r.at[part, h]
            )
            sends[ATT + part, k].start()

    locals_[6].wait()
    scan_r[h] = scan_s[h]
    arrive(SCAN)
    squares = jnp.zeros((TOK, 1), F32)
    for u in range(NX):
        z_in = gate_v[:, pl.ds(u * GW, GW)].astype(F32)
        gated = scan_r[u].astype(F32) * (z_in / (1.0 + jnp.exp(-z_in)))
        squares = squares + jnp.sum(gated * gated, axis=1, keepdims=True)
    inverse = lax.rsqrt(squares / MI + EPSILON)
    for u in range(NX):
        z_in = gate_v[:, pl.ds(u * GW, GW)].astype(F32)
        gated = scan_r[u].astype(F32) * (z_in / (1.0 + jnp.exp(-z_in)))
        normed = gated * inverse * norm_gain[:, pl.ds(u * GW, GW)]
        out[:, pl.ds(QH * HD + u * GW, GW)] = normed.astype(BF16)

    for part in range(PARTS):
        att_r[part, h] = att_s[part, h]
        lse_r[part, h] = lse_s[part, h]
        arrive(LSE + part)
        arrive(ATT + part)
        lse_all = lse_r[part].reshape(32, TOK).T
        for group in range(2):
            a, b = 2 * group, 2 * group + 1
            for i in range(per):
                one = lse_all[:, a * 8 + i : a * 8 + i + 1]
                two = lse_all[:, b * 8 + i : b * 8 + i + 1]
                cols = pl.ds(i * HD, HD)
                joined = att_r[part, a, :, cols].astype(F32) * (own_mask / (1.0 + jnp.exp2(two - one)))
                joined = joined + att_r[part, b, :, cols].astype(F32) * (
                    own_mask / (1.0 + jnp.exp2(one - two))
                )
                out[:, pl.ds(group * GW + (part * per + i) * HD, HD)] = joined.astype(BF16)

    for copy in sends.values():
        copy.wait_send()
    pltpu.make_async_remote_copy(
        src_ref=pool.at[pl.ds(0, NDP - 1)],
        dst_ref=pages.at[pl.ds(0, NDP - 1)],
        send_sem=page_send,
        recv_sem=page_recv.at[0],
        device_id=(d, (h + 1) % NX),
        device_id_type=MESH,
    ).wait_send()


def local(
    queries, fresh_keyvals, ssm_input, gate_input, state_maps, step_logit, slot_mask, cache_pool,
    page_map, cached_lengths, prior_state, decay_log, step_bias, skip_gain, norm_gain,
):
    hbm = pl.BlockSpec(memory_space=pl.ANY)
    vmem = pl.BlockSpec(memory_space=pltpu.VMEM)
    smem = pl.BlockSpec(memory_space=pltpu.SMEM)
    return pl.pallas_call(
        kernel,
        out_shape=pltpu.VMEM((TOK, QH * HD + MI), BF16),
        in_specs=[
            hbm, hbm, hbm, hbm, hbm, vmem, vmem, hbm, vmem, vmem, hbm, smem, smem, smem, vmem,
        ],
        out_specs=vmem,
        scratch_shapes=[
            pltpu.VMEM((TOK, 128), BF16),
            pltpu.VMEM((NX, TOK, 128), BF16),
            pltpu.VMEM((NX, TOK, 2 * STATE), BF16),
            pltpu.VMEM((NX, TOK, GW), BF16),
            pltpu.VMEM((NX, 32, 2 * HD), BF16),
            pltpu.VMEM((NX, TOK, GW), BF16),
            pltpu.VMEM((NDP, 8, 2 * HD), BF16),
            pltpu.VMEM((GW, STATE), BF16),
            pltpu.VMEM((TOK, MI), BF16),
            pltpu.VMEM((NX, TOK, GW), BF16),
            pltpu.VMEM((NX, TOK, GW), BF16),
            pltpu.VMEM((PARTS, NX, TOK, GW // PARTS), BF16),
            pltpu.VMEM((PARTS, NX, TOK, GW // PARTS), BF16),
            pltpu.VMEM((PARTS, NX, 8, TOK), F32),
            pltpu.VMEM((PARTS, NX, 8, TOK), F32),
            pltpu.VMEM((6, SPAN, HD), F32),
            pltpu.VMEM((CACHED + FRESH, HD), BF16),
            pltpu.VMEM((CACHED + FRESH, HD), BF16),
            pltpu.SemaphoreType.DMA((KINDS, NX)),
            pltpu.SemaphoreType.DMA((KINDS, NX)),
            pltpu.SemaphoreType.DMA,
            pltpu.SemaphoreType.DMA((2,)),
            pltpu.SemaphoreType.DMA((6,)),
            pltpu.SemaphoreType.REGULAR,
            pltpu.SemaphoreType.REGULAR,
        ],
        compiler_params=pltpu.CompilerParams(collective_id=0, has_side_effects=True),
        name="mixer",
    )(
        queries, fresh_keyvals, ssm_input, gate_input, state_maps, step_logit.T,
        slot_mask.reshape(1, TOK), cache_pool, page_map, cached_lengths.reshape(1, 1),
        prior_state.reshape(GW, STATE), decay_log, step_bias, skip_gain, norm_gain.reshape(1, MI),
    )


def solution(mesh):
    tokens = P(("dp", "head"), None)
    in_specs = (
        tokens, tokens, tokens, tokens, tokens, tokens,
        P(("dp", "head")),
        P("dp", "head", None),
        P("dp", None),
        P("dp"),
        P("dp", "head", None, None),
        P("head"), P("head"), P("head"),
        P(),
    )
    return jax.shard_map(
        local, mesh=mesh, in_specs=in_specs, out_specs=tokens, check_vma=False
    )
```
